256 devices in a mesh: dom: 32 (over x, z), load: 8 (over y, core).
Axes of the slice: x: 4, y: 4, z: 8, core: 2. Of those that a mesh axis runs over, the one named last changes fastest.
Arguments:
- load_current: float32 [8, 49152], P('load', 'dom'), may hold values from 0.1 to 1
- worst_node: int32 [8], P('load'), may hold values from 0 to 49151
- cond_diag: float32 [49152], P('dom'), may hold values from 0.5 to 4
- branch: float32 [384, 128, 128], P('dom'), may hold values from -0.5 to 0.5
- precond_factor: float32 [384, 128, 128], P('dom'), may hold values from -0.5 to 0.5
- coupling: float32 [5, 384, 128, 128], P(None, 'dom'), may hold values from -0.5 to 0.5
- sep_map: int32 [5, 384], P(None, 'dom'), may hold values from 0 to 11
- strap_ends: int32 [2, 524288], P(None, 'dom'), may hold values from 0 to 1535
Outputs:
- voltages: float32 [2, 8, 49152], P(None, 'load', 'dom')
- strap_grad: float32 [524288], P('dom')
The draws below stay inside these ranges and needn't reach their ends.
Inputs may be any that keep to these rules, and one draw needn't show every extreme that they name: `sep_map`: each entry names an interior block of the same partition as the separator block. `strap_ends`: both ends of a strap lie in the partition that holds the strap. `worst_node`: a global node index.
All inputs are finite; a program needn't handle non-finite values.
Results may differ from the reference program's by a relative error of at most 0.00017.
Values sent between devices are 32-bit elements; how exact they have to be, the bound alone decides.
No kernel may reach another device: no remote copies, remote signals or barrier semaphores. Data moves between devices by JAX's collectives and lax.ppermute only.
A program may use at most 128 MiB of HBM per device.

```python
import math
import jax
import jax.numpy as jnp
from jax import lax

BLK = 128
NBLK = 12
STRAP_DEV = 16384
ITERS = 4
LEVELS = 5
NI = 1536
NODES = 49152
TIMES = 8
STRAPS = 524288
N_DOM = 32


def set_ends(entries, key, low, largest):
    longest = entries.shape.index(max(entries.shape))
    spots = []
    for shift in (0, 1):
        where = [jax.random.randint(jax.random.fold_in(key, axis), (), 0, length) for axis, length in enumerate(entries.shape)]
        where[longest] = (where[longest] + shift) % entries.shape[longest]
        spots.append(tuple(where))
    return entries.at[spots[0]].set(low).at[spots[1]].set(largest)


def levels(rng, dims, shards, least, top_value):
    factor_of, own = 1.0, jax.random.fold_in(rng, 6)
    for dim, parts in shards:
        draws = jnp.exp(jax.random.uniform(jax.random.fold_in(own, dim), (parts,), jnp.float32, least / len(shards), top_value / len(shards)))
        factor_of = factor_of * jnp.repeat(draws, dims[dim] // parts).reshape([-1 if axis == dim else 1 for axis in range(len(dims))])
    return factor_of


def noise(own_key, shape, spread, bound, split=(), kind=jnp.bfloat16):
    factor_of = levels(own_key, shape, split, -0.22, 0.18) if split else 1.0
    values = jax.random.normal(own_key, shape, jnp.float32) * spread * factor_of
    return jnp.minimum(jnp.maximum(values, -bound), bound).astype(kind)


def setup_inputs(seed: int = 0) -> dict:
    streams_of = jax.random.split(jax.random.key(seed), 9)
    return {
        "load_current": jnp.clip(jnp.exp(math.log(1.0) - 2.3025851 * jax.random.uniform(streams_of[0], (TIMES, NODES), jnp.float32) ** levels(streams_of[0], (TIMES, NODES), ((0, 8), (1, 32)), -0.2, 0.2)), 0.1, 1.0),
        "worst_node": set_ends(jax.random.randint(streams_of[1], (TIMES,), 0, NODES), jax.random.fold_in(streams_of[1], 1), 0, NODES - 1).astype(jnp.int32),
        "cond_diag": jnp.clip(jnp.exp(math.log(4.0) - 2.0794415 * jax.random.uniform(streams_of[2], (NODES,), jnp.float32) ** levels(streams_of[2], (NODES,), ((0, 32),), -0.2, 0.2)), 0.5, 4.0),
        "branch": noise(streams_of[3], (N_DOM * NBLK, BLK, BLK), BLK ** -0.5, 0.5, ((0, 32),), jnp.float32),
        "precond_factor": noise(streams_of[4], (N_DOM * NBLK, BLK, BLK), BLK ** -0.5, 0.5, ((0, 32),), jnp.float32),
        "coupling": noise(streams_of[5], (LEVELS, N_DOM * NBLK, BLK, BLK), BLK ** -0.5, 0.5, ((1, 32),), jnp.float32),
        "sep_map": set_ends(jax.random.randint(streams_of[6], (LEVELS, N_DOM * NBLK), 0, NBLK), jax.random.fold_in(streams_of[6], 1), 0, NBLK - 1).astype(jnp.int32),
        "strap_ends": set_ends(jax.random.randint(streams_of[7], (2, STRAPS), 0, NI), jax.random.fold_in(streams_of[7], 1), 0, NI - 1).astype(jnp.int32),
    }


HIGHEST = lax.Precision.HIGHEST

def tree_sums(contrib):
    columns = contrib.shape[1]
    result = []
    for level_no in range(LEVELS):
        group = 2 ** (level_no + 1)
        shaped = contrib[level_no].reshape(columns, N_DOM // group, group, NBLK, BLK)
        summed = lax.optimization_barrier(jnp.sum(shaped, axis=2, keepdims=True))
        result.append(jnp.broadcast_to(summed, shaped.shape).reshape(columns, N_DOM * NBLK, BLK))
    return jnp.stack(result)

def coarse_part(blocks, coupling, global_map, level_weights):
    selected = jnp.stack([blocks[:, global_map[level_no]] for level_no in range(LEVELS)])
    contrib = jnp.einsum('ljmn,lrjn->lrjm', coupling, selected, precision=HIGHEST)
    group_sums = tree_sums(contrib)
    returned = jnp.einsum('ljmn,lrjm->lrjn', coupling, group_sums, precision=HIGHEST)
    result = jnp.zeros_like(blocks)
    for level_no in range(LEVELS):
        result = result.at[:, global_map[level_no]].add(level_weights[level_no] * returned[level_no])
    return result

def factor_apply(factor, blocks):
    inner = jnp.einsum('jnk,rjn->rjk', factor, blocks, precision=HIGHEST)
    return jnp.einsum('jnk,rjk->rjn', factor, inner, precision=HIGHEST)

def reference(load_current, worst_node, cond_diag, branch, precond_factor, coupling, sep_map, strap_ends):
    blocks_all = N_DOM * NBLK
    owners = jnp.arange(blocks_all, dtype=jnp.int32) // NBLK * NBLK
    global_map = (sep_map + owners[None, :]).astype(jnp.int32)
    shunt = cond_diag.reshape(blocks_all, BLK)
    node_ids = jnp.arange(NODES, dtype=jnp.int32)
    adjoint_rhs = (node_ids[None, :] == worst_node[:, None]).astype(jnp.float32)
    sources = jnp.concatenate([load_current, adjoint_rhs], 0).reshape(2 * TIMES, blocks_all, BLK)
    op_weights = [1.0 / math.sqrt(2.0 ** (level_no + 1)) for level_no in range(LEVELS)]
    pre_weights = [0.5 * value for value in op_weights]

    def apply_operator(blocks):
        return shunt * blocks + factor_apply(branch, blocks) + coarse_part(blocks, coupling, global_map, op_weights)

    def apply_precond(blocks):
        return blocks / (shunt + 1.0) + 0.25 * factor_apply(precond_factor, blocks) + coarse_part(blocks, coupling, global_map, pre_weights)

    def inner_sum(first, second):
        return lax.optimization_barrier(jnp.sum(first * second, axis=(1, 2)))
    solution = jnp.zeros_like(sources)
    residual = sources
    precond_res = apply_precond(residual)
    rho_now = inner_sum(residual, precond_res)
    direction = precond_res
    for iteration in range(ITERS):
        mapped = apply_operator(direction)
        step_size = rho_now / inner_sum(direction, mapped)
        solution = solution + step_size[:, None, None] * direction
        residual = residual - step_size[:, None, None] * mapped
        if iteration + 1 < ITERS:
            precond_res = apply_precond(residual)
            rho_new = inner_sum(residual, precond_res)
            direction = precond_res + (rho_new / rho_now)[:, None, None] * direction
            rho_now = rho_new
    voltages = solution.reshape(2, TIMES, NODES)
    strap_owner = jnp.arange(STRAPS, dtype=jnp.int32) // STRAP_DEV * NI
    strap_nodes = (strap_ends + strap_owner[None, :]).astype(jnp.int32)
    forward = voltages[0]
    adjoint = voltages[1]
    drop_diff = forward[:, strap_nodes[0]] - forward[:, strap_nodes[1]]
    adj_diff = adjoint[:, strap_nodes[0]] - adjoint[:, strap_nodes[1]]
    strap_grad = -lax.optimization_barrier(jnp.sum(adj_diff * drop_diff, axis=0))
    return (voltages, strap_grad)
```

```python
import math

import jax
import jax.numpy as jnp
from jax import lax
from jax.experimental import pallas as pl
from jax.experimental.pallas import tpu as pltpu
from jax.sharding import PartitionSpec as P

ITERS = 4
LEVELS = 5
NB = 12
W = 128
ROWS = 2 * NB
OP = [1.0 / math.sqrt(2.0 ** (level + 1)) for level in range(LEVELS)]
PRE = [0.5 * c for c in OP]
F32 = jnp.float32
BF16 = jnp.bfloat16
VMEM = pl.BlockSpec(memory_space=pltpu.VMEM)
SMEM = pl.BlockSpec(memory_space=pltpu.SMEM)
PARAMS = pltpu.CompilerParams(vmem_limit_bytes=40 * 1024 * 1024)


def split_rows(tile):
    high = tile.astype(BF16).astype(F32)
    return jnp.concatenate([high, tile - high], axis=0).astype(BF16)


def times(rows, matrix):
    out = lax.dot_general(
        jnp.concatenate([rows, rows], axis=1),
        matrix,
        (((1,), (0,)), ((), ())),
        preferred_element_type=F32,
    )
    return out[:8] + out[8:]


def times_t(rows, matrix):
    out = lax.dot_general(rows, matrix, (((1,), (1,)), ((), ())), preferred_element_type=F32)
    out = out[:8] + out[8:]
    return out[:, :W] + out[:, W:]


def split_kernel(mat_ref, out_ref):
    mats = mat_ref[...]
    high = mats.astype(BF16)
    out_ref[:, :W, :] = high
    out_ref[:, W:, :] = (mats - high.astype(F32)).astype(BF16)


def split_matrices(mats):
    count = mats.shape[0]
    step = 12
    return pl.pallas_call(
        split_kernel,
        grid=(count // step,),
        in_specs=[pl.BlockSpec((step, W, W), lambda i: (i, 0, 0))],
        out_specs=pl.BlockSpec((step, 2 * W, W), lambda i: (i, 0, 0)),
        out_shape=jax.ShapeDtypeStruct((count, 2 * W, W), BF16),
        compiler_params=PARAMS,
        name="split_matrices",
    )(mats)


def side_totals(square):
    total = square[0:8] + square[8:16] + square[16:24]
    total = total + pltpu.roll(total, 2, 0)
    total = total + pltpu.roll(total, 4, 0)
    return jnp.broadcast_to(jnp.sum(total, axis=1, keepdims=True), (8, W))


def coarse_back(sums, weights, coupling, sep, part, acc):
    for level in range(LEVELS):
        for group in range(NB // 4):
            rows = split_rows(sums[level][8 * group : 8 * group + 8, :] * weights[level])
            for member in range(4):
                j = 4 * group + member
                out = times(rows, coupling[level * NB + j])
                part[level * NB + j] = out if member == 0 else pltpu.roll(out, 8 - 2 * member, 0)
    acc[...] = jnp.zeros((NB, 8, W), F32)
    for level in range(LEVELS):
        for j in range(NB):
            k = sep[level, j]
            acc[k] = acc[k] + part[level * NB + j]


def local_part(vec, diag, scale, factor, coupling, sep, split, payload, applied):
    for k in range(NB):
        split[k] = split_rows(vec[k])
    for level in range(LEVELS):
        for j in range(NB):
            out = times_t(split[sep[level, j]], coupling[level * NB + j])
            payload[level * ROWS + 2 * j : level * ROWS + 2 * j + 2, :] = out[0:2]
    for k in range(NB):
        inner = times(split[k], factor[k])
        scaled = diag[k] * vec[k]
        square = scaled * vec[k] + scale * (inner * inner)
        payload[LEVELS * ROWS + 2 * k : LEVELS * ROWS + 2 * k + 2, :] = square[0:2]
        applied[k] = scaled + scale * times_t(split_rows(inner), factor[k])


def first_kernel(sep, vec, shunt, factor, coupling, payload, applied, split):
    v = [vec[k] for k in range(NB)]
    d = [1.0 / (shunt[k] + 1.0) for k in range(NB)]
    local_part(v, d, 0.25, factor, coupling, sep, split, payload, applied)


def keep_sides(tile):
    return jnp.where(lax.broadcasted_iota(jnp.int32, (8, W), 0) < 2, tile, 0.0)


def make_precond_kernel(first):
    def kernel(sep, *refs):
        sums = refs[:LEVELS]
        refs = refs[LEVELS:]
        if first:
            square, applied, shunt, factor, coupling, payload, next_applied, direction, rho, split, part, acc = refs
        else:
            (square, applied, shunt, factor, coupling, old_direction, old_rho) = refs[:7]
            payload, next_applied, direction, rho, split, part, acc = refs[7:]
        coarse_back(sums, PRE, coupling, sep, part, acc)
        rho_new = side_totals(square)
        if not first:
            ratio = rho_new / old_rho[...]
        rho[...] = rho_new
        vec = []
        for k in range(NB):
            tile = applied[k] + acc[k]
            if not first:
                tile = tile + ratio * old_direction[k]
            tile = keep_sides(tile)
            direction[k] = tile
            vec.append(tile)
        d = [shunt[k] for k in range(NB)]
        local_part(vec, d, 1.0, factor, coupling, sep, split, payload, next_applied)

    return kernel


def make_operator_kernel(first):
    def kernel(sep, *refs):
        sums = refs[:LEVELS]
        refs = refs[LEVELS:]
        square, applied, shunt, factor, coupling, direction, residual, rho = refs[:8]
        refs = refs[8:]
        if not first:
            estimate = refs[0]
            refs = refs[1:]
        payload, next_applied, next_residual, next_estimate, split, part, acc = refs
        coarse_back(sums, OP, coupling, sep, part, acc)
        step = rho[...] / side_totals(square)
        vec = []
        for k in range(NB):
            gain = step * direction[k]
            next_estimate[k] = gain if first else estimate[k] + gain
            tile = keep_sides(residual[k] - step * (applied[k] + acc[k]))
            next_residual[k] = tile
            vec.append(tile)
        d = [1.0 / (shunt[k] + 1.0) for k in range(NB)]
        local_part(vec, d, 0.25, factor, coupling, sep, split, payload, next_applied)

    return kernel


def last_kernel(square, direction, rho, estimate, ends, volts, terms):
    step = rho[...] / side_totals(square)
    for k in range(NB):
        tile = estimate[k] + step * direction[k]
        volts[0, k : k + 1, :] = tile[0:1]
        volts[1, k : k + 1, :] = tile[1:2]

    def chunk(i, carry):
        def drops(side):
            def at(end):
                index = ends[end, pl.ds(pl.multiple_of(8 * i, 8), 8), :]
                block = index >> 7
                lane = index & (W - 1)
                value = jnp.zeros((8, W), F32)
                for k in range(NB):
                    row = jnp.broadcast_to(volts[side, k : k + 1, :], (8, W))
                    value = jnp.where(block == k, jnp.take_along_axis(row, lane, axis=1), value)
                return value

            return at(0) - at(1)

        terms[pl.ds(pl.multiple_of(8 * i, 8), 8), :] = -(drops(1) * drops(0))
        return carry

    lax.fori_loop(0, terms.shape[0] // 8, chunk, 0)


TILES = jax.ShapeDtypeStruct((NB, 8, W), F32)
PAYLOAD = jax.ShapeDtypeStruct(((LEVELS + 1) * ROWS, W), F32)
TILE = jax.ShapeDtypeStruct((8, W), F32)
SPLIT = pltpu.VMEM((NB, 16, W), BF16)
PART = pltpu.VMEM((LEVELS * NB, 8, W), F32)
ACC = pltpu.VMEM((NB, 8, W), F32)


def call(kernel, name, args, outs, scratch, first_smem=True):
    return pl.pallas_call(
        kernel,
        in_specs=[SMEM if first_smem and i == 0 else VMEM for i in range(len(args))],
        out_specs=[VMEM] * len(outs),
        out_shape=outs,
        scratch_shapes=scratch,
        compiler_params=PARAMS,
        name=name,
    )(*args)


def tree_partners(level, count):
    half = 2**level
    if level == 2:
        inside = {0: 6, 1: 7, 2: 4, 3: 5, 4: 2, 5: 3, 6: 0, 7: 1}
        return [(s, s // 8 * 8 + inside[s % 8]) for s in range(count)]
    if level == 4:
        return [(s, (3 - s // 8) * 8 + s % 8) for s in range(count)]
    return [(s, s ^ half) for s in range(count)]


def tree_exchange(payload, weights):
    count = lax.axis_size("dom")
    pending = payload
    finished = []
    for level in range(LEVELS):
        pending = pending + lax.ppermute(pending, "dom", tree_partners(level, count))
        done = pending[:ROWS]
        finished.append(done)
        square = pending[-ROWS:] + weights[level] * (done * done)
        if level + 1 < LEVELS:
            pending = jnp.concatenate([pending[ROWS:-ROWS], square], axis=0)
    return finished, square


def shards(
    load_current, worst_node, cond_diag, branch, precond_factor, coupling, sep_map, strap_ends
):
    node_count = NB * W
    shunt = jnp.broadcast_to(cond_diag.reshape(NB, 1, W), (NB, 8, W))
    node_ids = lax.axis_index("dom") * node_count + jnp.arange(node_count, dtype=jnp.int32)
    adjoint = (node_ids == worst_node[0]).astype(F32).reshape(NB, 1, W)
    sources = jnp.concatenate(
        [load_current.reshape(NB, 1, W), adjoint, jnp.zeros((NB, 6, W), F32)], axis=1
    )
    ends = strap_ends.reshape(2, -1, W)
    cpl = split_matrices(coupling.reshape(LEVELS * NB, W, W))
    pre = split_matrices(precond_factor)
    brn = split_matrices(branch)

    payload, applied = call(
        first_kernel, "first_part", (sep_map, sources, shunt, pre, cpl), [PAYLOAD, TILES], [SPLIT]
    )
    residual = sources
    direction = rho = estimate = None
    for iteration in range(ITERS):
        first = iteration == 0
        sums, square = tree_exchange(payload, PRE)
        args = (sep_map, *sums, square, applied, shunt, brn, cpl)
        if not first:
            args += (direction, rho)
        payload, applied, direction, rho = call(
            make_precond_kernel(first),
            "precond_round",
            args,
            [PAYLOAD, TILES, TILES, TILE],
            [SPLIT, PART, ACC],
        )
        sums, square = tree_exchange(payload, OP)
        if iteration + 1 < ITERS:
            args = (sep_map, *sums, square, applied, shunt, pre, cpl, direction, residual, rho)
            if not first:
                args += (estimate,)
            payload, applied, residual, estimate = call(
                make_operator_kernel(first),
                "operator_round",
                args,
                [PAYLOAD, TILES, TILES, TILES],
                [SPLIT, PART, ACC],
            )
    volts, terms = call(
        last_kernel,
        "straps",
        (square, direction, rho, estimate, ends),
        [
            jax.ShapeDtypeStruct((2, NB, W), F32),
            jax.ShapeDtypeStruct(ends.shape[1:], F32),
        ],
        [],
        first_smem=False,
    )
    for pairs in (
        [(s, s ^ 1) for s in range(8)],
        [(s, s ^ 2) for s in range(8)],
        [(s, (3 - s // 2) * 2 + s % 2) for s in range(8)],
    ):
        terms = terms + lax.ppermute(terms, "load", pairs)
    return (volts.reshape(2, 1, node_count), terms.reshape(-1))


def solution(mesh):
    placed = (
        P("load", "dom"),
        P("load"),
        P("dom"),
        P("dom", None, None),
        P("dom", None, None),
        P(None, "dom", None, None),
        P(None, "dom"),
        P(None, "dom"),
    )
    return jax.shard_map(
        shards,
        mesh=mesh,
        in_specs=placed,
        out_specs=(P(None, "load", "dom"), P("dom")),
        check_vma=False,
    )
```

```python
import math

import jax
import jax.numpy as jnp
from jax import lax
from jax.experimental import pallas as pl
from jax.experimental.pallas import tpu as pltpu
from jax.sharding import PartitionSpec as P

ITERS = 4
LEVELS = 5
NB = 12
W = 128
ROWS = 2 * NB
OP = [1.0 / math.sqrt(2.0 ** (level + 1)) for level in range(LEVELS)]
PRE = [0.5 * c for c in OP]
F32 = jnp.float32
BF16 = jnp.bfloat16
VMEM = pl.BlockSpec(memory_space=pltpu.VMEM)
SMEM = pl.BlockSpec(memory_space=pltpu.SMEM)
HBM = pl.BlockSpec(memory_space=pltpu.HBM)
PARAMS = pltpu.CompilerParams(vmem_limit_bytes=40 * 1024 * 1024)


def split_rows(tile):
    high = tile.astype(BF16).astype(F32)
    return jnp.concatenate([high, tile - high], axis=0).astype(BF16)


def times(rows, matrix):
    out = lax.dot_general(
        jnp.concatenate([rows, rows], axis=1),
        matrix,
        (((1,), (0,)), ((), ())),
        preferred_element_type=F32,
    )
    return out[:8] + out[8:]


def times_t(rows, matrix):
    out = lax.dot_general(rows, matrix, (((1,), (1,)), ((), ())), preferred_element_type=F32)
    out = out[:8] + out[8:]
    return out[:, :W] + out[:, W:]


def store_split(mats, out, index):
    high = mats.astype(BF16)
    out[index, :W, :] = high
    out[index, W:, :] = (mats - high.astype(F32)).astype(BF16)


def split_kernel(mat_ref, out_ref):
    for j in range(NB):
        store_split(mat_ref[j], out_ref, j)


def transpose_kernel(coupling, flipped):
    row = lax.broadcasted_iota(jnp.int32, (W, W), 0)
    eye = (row == lax.broadcasted_iota(jnp.int32, (W, W), 1)).astype(F32).astype(BF16)
    for i in range(LEVELS * NB):
        out = lax.dot_general(
            eye, coupling[i], (((1,), (1,)), ((), ())), preferred_element_type=F32
        ).astype(BF16)
        flipped[i, :W, :] = out[:, :W]
        flipped[i, W:, :] = out[:, W:]


def side_totals(square):
    total = square[...]
    total = total + pltpu.roll(total, 2, 0)
    total = total + pltpu.roll(total, 4, 0)
    return jnp.broadcast_to(jnp.sum(total, axis=1, keepdims=True), (8, W))


def keep_sides(tile):
    return jnp.where(lax.broadcasted_iota(jnp.int32, (8, W), 0) < 2, tile, 0.0)


def coarse_back(levels, sums, weights, coupling, sep, acc):
    for level, total in zip(levels, sums):
        for group in range(NB // 4):
            rows = split_rows(total[8 * group : 8 * group + 8, :] * weights[level])
            for member in range(4):
                j = 4 * group + member
                out = times(rows, coupling[level * NB + j])
                if member:
                    out = pltpu.roll(out, 8 - 2 * member, 0)
                k = sep[level, j]
                acc[k] = acc[k] + out


def local_square(vec, diag, scale, factor, split, inner_out):
    square = jnp.zeros((8, W), F32)
    for k in range(NB):
        inner = times(split[k], factor[k])
        inner_out[k] = split_rows(inner)
        square = square + (diag[k] * vec[k] * vec[k] + scale * (inner * inner))
    return square


def contributions(multiply, levels, coupling, sep, split, payload):
    for level in levels:
        for j in range(NB):
            out = multiply(split[sep[level, j]], coupling[level * NB + j])
            payload[level * ROWS + 2 * j : level * ROWS + 2 * j + 2, :] = out[0:2]


def pre_diag(shunt):
    return [1.0 / (shunt[k] + 1.0) for k in range(NB)]


def first_kernel(
    sep, vec, shunt, coupling_hbm, factor_hbm, payload, inner_out, coupling, factor, raw, raw_factor, split, sems
):
    copies = [
        pltpu.make_async_copy(
            coupling_hbm.at[pl.ds(level * NB, NB)], raw.at[pl.ds(level * NB, NB)], sems.at[level]
        )
        for level in range(LEVELS)
    ]
    factor_copy = pltpu.make_async_copy(factor_hbm, raw_factor, sems.at[LEVELS])
    for copy in copies:
        copy.start()
    factor_copy.start()
    for k in range(NB):
        split[k] = split_rows(vec[k])
    for level in range(LEVELS):
        copies[level].wait()
        for j in range(NB):
            store_split(raw[level * NB + j], coupling, level * NB + j)
        contributions(times_t, [level], coupling, sep, split, payload)
    factor_copy.wait()
    for k in range(NB):
        store_split(raw_factor[k], factor, k)
    payload[LEVELS * ROWS :, :] = local_square(vec, pre_diag(shunt), 0.25, factor, split, inner_out)


def make_early_kernel(precond):
    def kernel(sep, sum0, sum1, vec, inner, shunt, factor, coupling, acc):
        diag = pre_diag(shunt) if precond else shunt
        scale = 0.25 if precond else 1.0
        for k in range(NB):
            acc[k] = diag[k] * vec[k] + scale * times_t(inner[k], factor[k])
        coarse_back([0, 1], [sum0, sum1], PRE if precond else OP, coupling, sep, acc)

    return kernel


def make_middle_kernel(precond):
    def kernel(sep, sum2, sum3, early, coupling, acc):
        acc[...] = early[...]
        coarse_back([2, 3], [sum2, sum3], PRE if precond else OP, coupling, sep, acc)

    return kernel


def make_precond_kernel(first):
    def kernel(sep, sum4, square, middle, shunt, factor, coupling, flipped, *refs):
        if not first:
            old_direction, old_rho = refs[:2]
            refs = refs[2:]
        payload, inner, direction, rho, split, acc = refs
        acc[...] = middle[...]
        coarse_back([4], [sum4], PRE, coupling, sep, acc)
        rho_new = side_totals(square)
        if not first:
            ratio = rho_new / old_rho[...]
        rho[...] = rho_new
        vec = []
        for k in range(NB):
            tile = acc[k]
            if not first:
                tile = tile + ratio * old_direction[k]
            tile = keep_sides(tile)
            direction[k] = tile
            split[k] = split_rows(tile)
            vec.append(tile)
        contributions(times, range(LEVELS), flipped, sep, split, payload)
        payload[LEVELS * ROWS :, :] = local_square(vec, shunt, 1.0, factor, split, inner)

    return kernel


def make_operator_kernel(first):
    def kernel(sep, sum4, square, middle, shunt, factor, coupling, flipped, *refs):
        direction, residual, rho = refs[:3]
        refs = refs[3:]
        if not first:
            estimate = refs[0]
            refs = refs[1:]
        payload, inner, next_residual, next_estimate, split, acc = refs
        acc[...] = middle[...]
        coarse_back([4], [sum4], OP, coupling, sep, acc)
        step = rho[...] / side_totals(square)
        vec = []
        for k in range(NB):
            tile = keep_sides(residual[k] - step * acc[k])
            next_residual[k] = tile
            split[k] = split_rows(tile)
            vec.append(tile)
        contributions(times, range(LEVELS), flipped, sep, split, payload)
        payload[LEVELS * ROWS :, :] = local_square(vec, pre_diag(shunt), 0.25, factor, split, inner)
        for k in range(NB):
            gain = step * direction[k]
            next_estimate[k] = gain if first else estimate[k] + gain

    return kernel


def drops_kernel(vec, ends, drops):
    def chunk(i, carry):
        here = pl.ds(pl.multiple_of(8 * i, 8), 8)

        def at(end):
            index = ends[end, here, :]
            block = index >> 7
            lane = index & (W - 1)
            values = [jnp.zeros((8, W), F32)] * 2
            for k in range(NB):
                chosen = block == k
                for side in range(2):
                    row = jnp.broadcast_to(vec[k, side : side + 1, :], (8, W))
                    found = jnp.take_along_axis(row, lane, axis=1)
                    values[side] = jnp.where(chosen, found, values[side])
            return values

        low, high = at(0), at(1)
        for side in range(2):
            drops[side, here, :] = low[side] - high[side]
        return carry

    lax.fori_loop(0, drops.shape[1] // 8, chunk, 0)


def last_kernel(square, direction, rho, estimate, known, change, volts, terms):
    step = rho[...] / side_totals(square)
    for side in range(2):
        gain = jnp.broadcast_to(step[side : side + 1, :], (8, W))
        if side == 0:
            forward = gain
        else:
            adjoint = gain
    for i in range(terms.shape[0] // 8):
        here = slice(8 * i, 8 * i + 8)
        drop = known[0, here, :] + forward * change[0, here, :]
        back = known[1, here, :] + adjoint * change[1, here, :]
        terms[here, :] = -(back * drop)
    for k in range(NB):
        tile = estimate[k] + step * direction[k]
        volts[0, k : k + 1, :] = tile[0:1]
        volts[1, k : k + 1, :] = tile[1:2]


TILES = jax.ShapeDtypeStruct((NB, 8, W), F32)
PAYLOAD = jax.ShapeDtypeStruct((LEVELS * ROWS + 8, W), F32)
TILE = jax.ShapeDtypeStruct((8, W), F32)
INNER = jax.ShapeDtypeStruct((NB, 16, W), BF16)
COUPLING = jax.ShapeDtypeStruct((LEVELS * NB, 2 * W, W), BF16)
FACTOR = jax.ShapeDtypeStruct((NB, 2 * W, W), BF16)
SPLIT = pltpu.VMEM((NB, 16, W), BF16)
ACC = pltpu.VMEM((NB, 8, W), F32)


def call(kernel, name, args, outs, scratch=(), smem=True, hbm=()):
    specs = [VMEM] * len(args)
    if smem:
        specs[0] = SMEM
    for i in hbm:
        specs[i] = HBM
    one = not isinstance(outs, list)
    return pl.pallas_call(
        kernel,
        in_specs=specs,
        out_specs=VMEM if one else [VMEM] * len(outs),
        out_shape=outs,
        scratch_shapes=list(scratch),
        compiler_params=PARAMS,
        name=name,
    )(*args)


def tree_partners(level, count):
    if level == 2:
        inside = {0: 6, 1: 7, 2: 4, 3: 5, 4: 2, 5: 3, 6: 0, 7: 1}
        return [(s, s // 8 * 8 + inside[s % 8]) for s in range(count)]
    return [(s, s ^ 2**level) for s in range(count)]


def tree_exchange(payload, weights, early, middle):
    count = lax.axis_size("dom")
    pending = payload
    finished = []
    partial = None
    for level in range(LEVELS):
        received = lax.ppermute(pending, "dom", tree_partners(level, count))
        if level == 2 and early is not None:
            partial = early(finished[0], finished[1])
        if level == 4 and early is not None:
            partial = middle(finished[2], finished[3], partial)
        pending = pending + received
        done = pending[:ROWS]
        finished.append(done)
        power = done[:8] * done[:8] + done[8:16] * done[8:16] + done[16:] * done[16:]
        square = pending[-8:] + weights[level] * power
        if level + 1 < LEVELS:
            pending = jnp.concatenate([pending[ROWS:-8], square], axis=0)
    return done, square, partial


def shards(
    load_current, worst_node, cond_diag, branch, precond_factor, coupling, sep_map, strap_ends
):
    node_count = NB * W
    shunt = jnp.broadcast_to(cond_diag.reshape(NB, 1, W), (NB, 8, W))
    node_ids = lax.axis_index("dom") * node_count + jnp.arange(node_count, dtype=jnp.int32)
    adjoint = (node_ids == worst_node[0]).astype(F32).reshape(NB, 1, W)
    sources = jnp.concatenate(
        [load_current.reshape(NB, 1, W), adjoint, jnp.zeros((NB, 6, W), F32)], axis=1
    )
    ends = strap_ends.reshape(2, -1, W)
    strap_rows = ends.shape[1]
    drops_shape = jax.ShapeDtypeStruct(ends.shape, F32)

    payload, inner, cpl, pre = call(
        first_kernel,
        "first_part",
        (sep_map, sources, shunt, coupling.reshape(LEVELS * NB, W, W), precond_factor),
        [PAYLOAD, INNER, COUPLING, FACTOR],
        [
            pltpu.VMEM((LEVELS * NB, W, W), F32),
            pltpu.VMEM((NB, W, W), F32),
            SPLIT,
            pltpu.SemaphoreType.DMA((LEVELS + 1,)),
        ],
        hbm=(3, 4),
    )
    flipped = call(transpose_kernel, "flip", (cpl,), COUPLING, smem=False)
    brn = call(split_kernel, "split_branch", (branch,), FACTOR, smem=False)
    residual = sources
    direction = rho = estimate = known = None

    def exchange(payload, precond, vec, inner, factor, last=False):
        def early(sum0, sum1):
            args = (sep_map, sum0, sum1, vec, inner, shunt, factor, cpl)
            return call(make_early_kernel(precond), "early_levels", args, TILES)

        def middle(sum2, sum3, partial):
            args = (sep_map, sum2, sum3, partial, cpl)
            return call(make_middle_kernel(precond), "middle_levels", args, TILES)

        weights = PRE if precond else OP
        return tree_exchange(payload, weights, None if last else early, None if last else middle)

    for iteration in range(ITERS):
        first = iteration == 0
        last = iteration + 1 == ITERS
        sum4, square, partial = exchange(payload, True, residual, inner, pre)
        if last:
            known = call(drops_kernel, "known_drops", (estimate, ends), drops_shape, smem=False)
        args = (sep_map, sum4, square, partial, shunt, brn, cpl, flipped)
        if not first:
            args += (direction, rho)
        payload, inner, direction, rho = call(
            make_precond_kernel(first),
            "precond_round",
            args,
            [PAYLOAD, INNER, TILES, TILE],
            [SPLIT, ACC],
        )
        if last:
            change = call(drops_kernel, "change_drops", (direction, ends), drops_shape, smem=False)
        sum4, square, partial = exchange(payload, False, direction, inner, brn, last)
        if not last:
            args = (sep_map, sum4, square, partial, shunt, pre, cpl, flipped)
            args += (direction, residual, rho)
            if not first:
                args += (estimate,)
            payload, inner, residual, estimate = call(
                make_operator_kernel(first),
                "operator_round",
                args,
                [PAYLOAD, INNER, TILES, TILES],
                [SPLIT, ACC],
            )
    volts, terms = call(
        last_kernel,
        "straps",
        (square, direction, rho, estimate, known, change),
        [
            jax.ShapeDtypeStruct((2, NB, W), F32),
            jax.ShapeDtypeStruct((strap_rows, W), F32),
        ],
        smem=False,
    )
    for mask in (1, 2, 4):
        terms = terms + lax.ppermute(terms, "load", [(s, s ^ mask) for s in range(8)])
    return (volts.reshape(2, 1, node_count), terms.reshape(-1))


def solution(mesh):
    placed = (
        P("load", "dom"),
        P("load"),
        P("dom"),
        P("dom", None, None),
        P("dom", None, None),
        P(None, "dom", None, None),
        P(None, "dom"),
        P(None, "dom"),
    )
    return jax.shard_map(
        shards,
        mesh=mesh,
        in_specs=placed,
        out_specs=(P(None, "load", "dom"), P("dom")),
        check_vma=False,
    )
```

```python
import math

import jax
import jax.numpy as jnp
from jax import lax
from jax.experimental import pallas as pl
from jax.experimental.pallas import tpu as pltpu
from jax.sharding import PartitionSpec as P

ITERS = 4
LEVELS = 5
NB = 12
W = 128
ROWS = 2 * NB
OP = [1.0 / math.sqrt(2.0 ** (level + 1)) for level in range(LEVELS)]
PRE = [0.5 * c for c in OP]
F32 = jnp.float32
BF16 = jnp.bfloat16
VMEM = pl.BlockSpec(memory_space=pltpu.VMEM)
SMEM = pl.BlockSpec(memory_space=pltpu.SMEM)
HBM = pl.BlockSpec(memory_space=pltpu.HBM)
MIB = 1024 * 1024


def split_rows(tile):
    high = tile.astype(BF16).astype(F32)
    return jnp.concatenate([high, tile - high], axis=0).astype(BF16)


def times(rows, matrix):
    out = lax.dot_general(
        jnp.concatenate([rows, rows], axis=1),
        matrix,
        (((1,), (0,)), ((), ())),
        preferred_element_type=F32,
    )
    return out[:8] + out[8:]


def times_t(rows, matrix):
    out = lax.dot_general(rows, matrix, (((1,), (1,)), ((), ())), preferred_element_type=F32)
    out = out[:8] + out[8:]
    return out[:, :W] + out[:, W:]


def store_split(mats, out, index):
    high = mats.astype(BF16)
    out[index, :W, :] = high
    out[index, W:, :] = (mats - high.astype(F32)).astype(BF16)


def split_kernel(mat_ref, out_ref):
    for j in range(NB):
        store_split(mat_ref[j], out_ref, j)


def transpose_kernel(coupling, flipped):
    row = lax.broadcasted_iota(jnp.int32, (W, W), 0)
    eye = (row == lax.broadcasted_iota(jnp.int32, (W, W), 1)).astype(F32).astype(BF16)
    for i in range(LEVELS * NB):
        out = lax.dot_general(
            eye, coupling[i], (((1,), (1,)), ((), ())), preferred_element_type=F32
        ).astype(BF16)
        flipped[i, :W, :] = out[:, :W]
        flipped[i, W:, :] = out[:, W:]


def side_totals(square):
    total = square[...]
    total = total + pltpu.roll(total, 2, 0)
    total = total + pltpu.roll(total, 4, 0)
    return jnp.broadcast_to(jnp.sum(total, axis=1, keepdims=True), (8, W))


def keep_sides(tile):
    return jnp.where(lax.broadcasted_iota(jnp.int32, (8, W), 0) < 2, tile, 0.0)


def coarse_back(levels, sums, weights, coupling, sep, acc):
    for level, total in zip(levels, sums):
        for group in range(NB // 4):
            rows = split_rows(total[8 * group : 8 * group + 8, :] * weights[level])
            for member in range(4):
                j = 4 * group + member
                out = times(rows, coupling[level * NB + j])
                if member:
                    out = pltpu.roll(out, 8 - 2 * member, 0)
                k = sep[level, j]
                acc[k] = acc[k] + out


def local_square(vec, diag, scale, factor, split, inner_out):
    square = jnp.zeros((8, W), F32)
    for k in range(NB):
        inner = times(split[k], factor[k])
        inner_out[k] = split_rows(inner)
        square = square + (diag[k] * vec[k] * vec[k] + scale * (inner * inner))
    return square


def contributions(multiply, levels, coupling, sep, split, payload):
    for level in levels:
        for j in range(NB):
            out = multiply(split[sep[level, j]], coupling[level * NB + j])
            payload[level * ROWS + 2 * j : level * ROWS + 2 * j + 2, :] = out[0:2]


def own_diag(shunt):
    return [jnp.broadcast_to(shunt[k : k + 1, :], (8, W)) for k in range(NB)]


def pre_diag(shunt):
    return [1.0 / (tile + 1.0) for tile in own_diag(shunt)]


def first_kernel(
    sep,
    target,
    load,
    shunt,
    coupling_hbm,
    factor_hbm,
    payload,
    inner_out,
    vec_out,
    coupling,
    factor,
    raw,
    raw_factor,
    split,
    sems,
):
    copies = [
        pltpu.make_async_copy(
            coupling_hbm.at[pl.ds(level * NB, NB)], raw.at[pl.ds(level * NB, NB)], sems.at[level]
        )
        for level in range(LEVELS)
    ]
    factor_copy = pltpu.make_async_copy(factor_hbm, raw_factor, sems.at[LEVELS])
    for copy in copies:
        copy.start()
    factor_copy.start()
    side = lax.broadcasted_iota(jnp.int32, (8, W), 0)
    lane = lax.broadcasted_iota(jnp.int32, (8, W), 1)
    vec = []
    for k in range(NB):
        unit = jnp.where((side == 1) & (lane + k * W == target[0]), 1.0, 0.0)
        row = jnp.broadcast_to(load[0:1, k * W : (k + 1) * W], (8, W))
        tile = jnp.where(side == 0, row, unit)
        vec_out[k] = tile
        split[k] = split_rows(tile)
        vec.append(tile)
    for level in range(LEVELS):
        copies[level].wait()
        for j in range(NB):
            store_split(raw[level * NB + j], coupling, level * NB + j)
        contributions(times_t, [level], coupling, sep, split, payload)
    factor_copy.wait()
    for k in range(NB):
        store_split(raw_factor[k], factor, k)
    payload[LEVELS * ROWS :, :] = local_square(vec, pre_diag(shunt), 0.25, factor, split, inner_out)


def make_early_kernel(precond):
    def kernel(sep, sum0, sum1, vec, inner, shunt, factor, coupling, acc):
        diag = pre_diag(shunt) if precond else own_diag(shunt)
        scale = 0.25 if precond else 1.0
        for k in range(NB):
            acc[k] = diag[k] * vec[k] + scale * times_t(inner[k], factor[k])
        coarse_back([0, 1], [sum0, sum1], PRE if precond else OP, coupling, sep, acc)

    return kernel


def make_middle_kernel(precond):
    def kernel(sep, sum2, sum3, early, coupling, acc):
        acc[...] = early[...]
        coarse_back([2, 3], [sum2, sum3], PRE if precond else OP, coupling, sep, acc)

    return kernel


def make_precond_kernel(first):
    def kernel(sep, sum4, square, middle, shunt, factor, coupling, flipped, *refs):
        if not first:
            old_direction, old_rho = refs[:2]
            refs = refs[2:]
        payload, inner, direction, rho, split, acc = refs
        acc[...] = middle[...]
        coarse_back([4], [sum4], PRE, coupling, sep, acc)
        rho_new = side_totals(square)
        if not first:
            ratio = rho_new / old_rho[...]
        rho[...] = rho_new
        vec = []
        for k in range(NB):
            tile = acc[k]
            if not first:
                tile = tile + ratio * old_direction[k]
            tile = keep_sides(tile)
            direction[k] = tile
            split[k] = split_rows(tile)
            vec.append(tile)
        contributions(times, range(LEVELS), flipped, sep, split, payload)
        payload[LEVELS * ROWS :, :] = local_square(vec, own_diag(shunt), 1.0, factor, split, inner)

    return kernel


def make_operator_kernel(first):
    def kernel(sep, sum4, square, middle, shunt, factor, coupling, flipped, *refs):
        direction, residual, rho = refs[:3]
        refs = refs[3:]
        if not first:
            estimate = refs[0]
            refs = refs[1:]
        payload, inner, next_residual, next_estimate, split, acc = refs
        acc[...] = middle[...]
        coarse_back([4], [sum4], OP, coupling, sep, acc)
        step = rho[...] / side_totals(square)
        vec = []
        for k in range(NB):
            tile = keep_sides(residual[k] - step * acc[k])
            next_residual[k] = tile
            split[k] = split_rows(tile)
            vec.append(tile)
        contributions(times, range(LEVELS), flipped, sep, split, payload)
        payload[LEVELS * ROWS :, :] = local_square(vec, pre_diag(shunt), 0.25, factor, split, inner)
        for k in range(NB):
            gain = step * direction[k]
            next_estimate[k] = gain if first else estimate[k] + gain

    return kernel


def drops_kernel(vec, ends, drops):
    def chunk(i, carry):
        here = pl.ds(pl.multiple_of(8 * i, 8), 8)

        def at(end):
            index = ends[end, here, :]
            block = index >> 7
            lane = index & (W - 1)
            values = [jnp.zeros((8, W), F32)] * 2
            for k in range(NB):
                chosen = block == k
                for side in range(2):
                    row = jnp.broadcast_to(vec[k, side : side + 1, :], (8, W))
                    found = jnp.take_along_axis(row, lane, axis=1)
                    values[side] = jnp.where(chosen, found, values[side])
            return values

        low, high = at(0), at(1)
        for side in range(2):
            drops[side, here, :] = low[side] - high[side]
        return carry

    lax.fori_loop(0, drops.shape[1] // 8, chunk, 0)


def last_kernel(square, direction, rho, estimate, known, change, volts, terms):
    step = rho[...] / side_totals(square)
    for side in range(2):
        gain = jnp.broadcast_to(step[side : side + 1, :], (8, W))
        if side == 0:
            forward = gain
        else:
            adjoint = gain
    for i in range(terms.shape[0] // 8):
        here = slice(8 * i, 8 * i + 8)
        drop = known[0, here, :] + forward * change[0, here, :]
        back = known[1, here, :] + adjoint * change[1, here, :]
        terms[here, :] = -(back * drop)
    for k in range(NB):
        tile = estimate[k] + step * direction[k]
        volts[0, k : k + 1, :] = tile[0:1]
        volts[1, k : k + 1, :] = tile[1:2]


TILES = jax.ShapeDtypeStruct((NB, 8, W), F32)
PAYLOAD = jax.ShapeDtypeStruct((LEVELS * ROWS + 8, W), F32)
TILE = jax.ShapeDtypeStruct((8, W), F32)
INNER = jax.ShapeDtypeStruct((NB, 16, W), BF16)
COUPLING = jax.ShapeDtypeStruct((LEVELS * NB, 2 * W, W), BF16)
FACTOR = jax.ShapeDtypeStruct((NB, 2 * W, W), BF16)
SPLIT = pltpu.VMEM((NB, 16, W), BF16)
ACC = pltpu.VMEM((NB, 8, W), F32)


def call(kernel, name, args, outs, scratch=(), smem=1, hbm=(), limit=16):
    specs = [SMEM if i < smem else HBM if i in hbm else VMEM for i in range(len(args))]
    one = not isinstance(outs, list)
    return pl.pallas_call(
        kernel,
        in_specs=specs,
        out_specs=VMEM if one else [VMEM] * len(outs),
        out_shape=outs,
        scratch_shapes=list(scratch),
        compiler_params=pltpu.CompilerParams(vmem_limit_bytes=limit * MIB),
        name=name,
    )(*args)


def tree_partners(level, count):
    if level == 2:
        inside = {0: 6, 1: 7, 2: 4, 3: 5, 4: 2, 5: 3, 6: 0, 7: 1}
        return [(s, s // 8 * 8 + inside[s % 8]) for s in range(count)]
    return [(s, s ^ 2**level) for s in range(count)]


def tree_exchange(payload, weights, jobs):
    count = lax.axis_size("dom")
    pending = payload
    finished = []
    results = {}
    for level in range(LEVELS):
        received = lax.ppermute(pending, "dom", tree_partners(level, count))
        if level in jobs:
            results[level] = jobs[level](finished, results)
            received, results[level] = lax.optimization_barrier((received, results[level]))
        pending = pending + received
        done = pending[:ROWS]
        finished.append(done)
        power = done[:8] * done[:8] + done[8:16] * done[8:16] + done[16:] * done[16:]
        square = pending[-8:] + weights[level] * power
        if level + 1 < LEVELS:
            pending = jnp.concatenate([pending[ROWS:-8], square], axis=0)
    return done, square, results


def shards(
    load_current, worst_node, cond_diag, branch, precond_factor, coupling, sep_map, strap_ends
):
    node_count = NB * W
    shunt = cond_diag.reshape(NB, W)
    target = worst_node - lax.axis_index("dom") * node_count
    ends = strap_ends.reshape(2, -1, W)
    strap_rows = ends.shape[1]
    drops_shape = jax.ShapeDtypeStruct(ends.shape, F32)

    payload, inner, residual, cpl, pre = call(
        first_kernel,
        "first_part",
        (
            sep_map,
            target,
            load_current,
            shunt,
            pltpu.with_memory_space_constraint(coupling.reshape(LEVELS * NB, W, W), pltpu.HBM),
            pltpu.with_memory_space_constraint(precond_factor, pltpu.HBM),
        ),
        [PAYLOAD, INNER, TILES, COUPLING, FACTOR],
        [
            pltpu.VMEM((LEVELS * NB, W, W), F32),
            pltpu.VMEM((NB, W, W), F32),
            SPLIT,
            pltpu.SemaphoreType.DMA((LEVELS + 1,)),
        ],
        smem=2,
        hbm=(4, 5),
        limit=24,
    )
    direction = rho = estimate = flipped = brn = None

    def exchange(payload, precond, vec, inner, factor, jobs, back=True):
        def early(finished, results):
            args = (sep_map, finished[0], finished[1], vec, inner, shunt, factor, cpl)
            return call(make_early_kernel(precond), "early_levels", args, TILES)

        def middle(finished, results):
            args = (sep_map, finished[2], finished[3], results[2], cpl)
            return call(make_middle_kernel(precond), "middle_levels", args, TILES)

        if back:
            jobs = {**jobs, 2: early, 4: middle}
        return tree_exchange(payload, PRE if precond else OP, jobs)

    for iteration in range(ITERS):
        first = iteration == 0
        last = iteration + 1 == ITERS
        jobs = {}
        if first:
            jobs[0] = lambda *_: call(split_kernel, "split_branch", (branch,), FACTOR, smem=0)
            jobs[1] = lambda *_: call(transpose_kernel, "flip", (cpl,), COUPLING, smem=0)
        if last:
            jobs[1] = lambda *_: call(drops_kernel, "known", (estimate, ends), drops_shape, smem=0)
        sum4, square, results = exchange(payload, True, residual, inner, pre, jobs)
        if first:
            brn, flipped = results[0], results[1]
        if last:
            known = results[1]
        args = (sep_map, sum4, square, results[4], shunt, brn, cpl, flipped)
        if not first:
            args += (direction, rho)
        payload, inner, direction, rho = call(
            make_precond_kernel(first),
            "precond_round",
            args,
            [PAYLOAD, INNER, TILES, TILE],
            [SPLIT, ACC],
        )
        jobs = {}
        if last:
            jobs[1] = lambda *_: call(drops_kernel, "change", (direction, ends), drops_shape, smem=0)
        sum4, square, results = exchange(payload, False, direction, inner, brn, jobs, not last)
        if last:
            change = results[1]
        else:
            args = (sep_map, sum4, square, results[4], shunt, pre, cpl, flipped)
            args += (direction, residual, rho)
            if not first:
                args += (estimate,)
            payload, inner, residual, estimate = call(
                make_operator_kernel(first),
                "operator_round",
                args,
                [PAYLOAD, INNER, TILES, TILES],
                [SPLIT, ACC],
            )
    volts, terms = call(
        last_kernel,
        "straps",
        (square, direction, rho, estimate, known, change),
        [
            jax.ShapeDtypeStruct((2, NB, W), F32),
            jax.ShapeDtypeStruct((strap_rows, W), F32),
        ],
        smem=0,
    )
    for mask in (1, 2, 4):
        terms = terms + lax.ppermute(terms, "load", [(s, s ^ mask) for s in range(8)])
    return (volts.reshape(2, 1, node_count), terms.reshape(-1))


def solution(mesh):
    placed = (
        P("load", "dom"),
        P("load"),
        P("dom"),
        P("dom", None, None),
        P("dom", None, None),
        P(None, "dom", None, None),
        P(None, "dom"),
        P(None, "dom"),
    )
    return jax.shard_map(
        shards,
        mesh=mesh,
        in_specs=placed,
        out_specs=(P(None, "load", "dom"), P("dom")),
        check_vma=False,
    )
```

```python
import math

import jax
import jax.numpy as jnp
from jax import lax
from jax.experimental import pallas as pl
from jax.experimental.pallas import tpu as pltpu
from jax.sharding import PartitionSpec as P

ITERS = 4
LEVELS = 5
NB = 12
W = 128
ROWS = 2 * NB
FLAT = 8 * NB
OP = [1.0 / math.sqrt(2.0 ** (level + 1)) for level in range(LEVELS)]
PRE = [0.5 * c for c in OP]
F32 = jnp.float32
BF16 = jnp.bfloat16
VMEM = pl.BlockSpec(memory_space=pltpu.VMEM)
SMEM = pl.BlockSpec(memory_space=pltpu.SMEM)
HBM = pl.BlockSpec(memory_space=pltpu.HBM)
MIB = 1024 * 1024


def split_rows(tile):
    high = tile.astype(BF16).astype(F32)
    return jnp.concatenate([high, tile - high], axis=0).astype(BF16)


def times(rows, matrix):
    out = lax.dot_general(
        jnp.concatenate([rows, rows], axis=1),
        matrix,
        (((1,), (0,)), ((), ())),
        preferred_element_type=F32,
    )
    return out[:8] + out[8:]


def times_t(rows, matrix):
    out = lax.dot_general(rows, matrix, (((1,), (1,)), ((), ())), preferred_element_type=F32)
    out = out[:8] + out[8:]
    return out[:, :W] + out[:, W:]


def store_split(mats, out, index):
    high = mats.astype(BF16)
    out[index, :W, :] = high
    out[index, W:, :] = (mats - high.astype(F32)).astype(BF16)


def split_kernel(mat_ref, out_ref):
    for j in range(NB):
        store_split(mat_ref[j], out_ref, j)


def transpose_kernel(coupling, flipped):
    row = lax.broadcasted_iota(jnp.int32, (W, W), 0)
    eye = (row == lax.broadcasted_iota(jnp.int32, (W, W), 1)).astype(F32).astype(BF16)
    for i in range(LEVELS * NB):
        out = lax.dot_general(
            eye, coupling[i], (((1,), (1,)), ((), ())), preferred_element_type=F32
        ).astype(BF16)
        flipped[i, :W, :] = out[:, :W]
        flipped[i, W:, :] = out[:, W:]


def side_totals(square):
    total = square[...]
    total = total + pltpu.roll(total, 2, 0)
    total = total + pltpu.roll(total, 4, 0)
    return jnp.broadcast_to(jnp.sum(total, axis=1, keepdims=True), (8, W))


def keep_sides(tile):
    return jnp.where(lax.broadcasted_iota(jnp.int32, (8, W), 0) < 2, tile, 0.0)


def tile_of(ref, k):
    return ref[8 * k : 8 * k + 8, :]


def stacked(values):
    high = values.astype(BF16).astype(F32)
    zeros = jnp.zeros((256 - 2 * FLAT, W), F32)
    return jnp.concatenate([high, values - high, zeros], axis=0).astype(BF16)


def dot(left, right):
    return lax.dot_general(left, right, (((1,), (0,)), ((), ())), preferred_element_type=F32)


def make_choices(sep, pick, place):
    row = lax.broadcasted_iota(jnp.int32, (16, 256), 0)
    col = lax.broadcasted_iota(jnp.int32, (16, 256), 1)
    start = jnp.where(row < 2, row, jnp.where((row >= 8) & (row < 10), FLAT - 8 + row, -4096))
    offset = col - start
    for level in range(LEVELS):
        for j in range(NB):
            i = level * NB + j
            pick[16 * i : 16 * i + 16, :] = jnp.where(offset == 8 * sep[level, j], 1.0, 0.0).astype(BF16)
    row = lax.broadcasted_iota(jnp.int32, (8, 256), 0)
    col = lax.broadcasted_iota(jnp.int32, (8, 256), 1)
    inside = jnp.where(col >= FLAT, col - FLAT, col)
    block = inside >> 3
    valid = (row < 2) & (col < 2 * FLAT) & ((inside & 7) == 2 * (block & 3) + row)
    for level in range(LEVELS):
        owner = jnp.full((8, 256), -1, jnp.int32)
        for j in range(NB):
            owner = jnp.where(valid & (block == j), sep[level, j], owner)
        tiles = [jnp.where(owner == k, 1.0, 0.0) for k in range(NB)]
        place[level] = jnp.concatenate(tiles, axis=0).astype(BF16)


def coarse_back(level, total, weights, coupling, place):
    outs = []
    for group in range(NB // 4):
        rows = split_rows(total[8 * group : 8 * group + 8, :] * weights[level])
        for member in range(4):
            outs.append(times(rows, coupling[level * NB + 4 * group + member]))
    return dot(place[level], stacked(jnp.concatenate(outs, axis=0)))


def local_square(vec, diag, scale, factor, inner_out):
    square = jnp.zeros((8, W), F32)
    for k in range(NB):
        inner = times(split_rows(vec[k]), factor[k])
        inner_out[k] = split_rows(inner)
        square = square + (diag[k] * vec[k] * vec[k] + scale * (inner * inner))
    return square


def put(payload, level, j, out):
    payload[level * ROWS + 2 * j : level * ROWS + 2 * j + 2, :] = out[0:2]


def contributions(vec, flipped, pick, payload):
    chosen = dot(pick[...], stacked(jnp.concatenate(vec, axis=0))).astype(BF16)
    for level in range(LEVELS):
        for j in range(NB):
            i = level * NB + j
            put(payload, level, j, times(chosen[16 * i : 16 * i + 16], flipped[i]))


def own_diag(shunt):
    return [jnp.broadcast_to(shunt[k : k + 1, :], (8, W)) for k in range(NB)]


def pre_diag(shunt):
    return [1.0 / (tile + 1.0) for tile in own_diag(shunt)]


def first_kernel(
    sep,
    target,
    load_hbm,
    shunt_hbm,
    coupling_hbm,
    factor_hbm,
    payload,
    inner_out,
    vec_out,
    coupling,
    factor,
    pick,
    place,
    load,
    shunt,
    raw,
    raw_factor,
    split,
    sems,
):
    copies = [
        pltpu.make_async_copy(
            coupling_hbm.at[pl.ds(level * NB, NB)], raw.at[pl.ds(level * NB, NB)], sems.at[level]
        )
        for level in range(LEVELS)
    ]
    factor_copy = pltpu.make_async_copy(factor_hbm, raw_factor, sems.at[LEVELS])
    load_copy = pltpu.make_async_copy(load_hbm, load, sems.at[LEVELS + 1])
    shunt_copy = pltpu.make_async_copy(shunt_hbm, shunt, sems.at[LEVELS + 2])
    load_copy.start()
    shunt_copy.start()
    for copy in copies:
        copy.start()
    factor_copy.start()
    make_choices(sep, pick, place)
    load_copy.wait()
    side = lax.broadcasted_iota(jnp.int32, (8, W), 0)
    lane = lax.broadcasted_iota(jnp.int32, (8, W), 1)
    vec = []
    for k in range(NB):
        unit = jnp.where((side == 1) & (lane + k * W == target[0]), 1.0, 0.0)
        row = jnp.broadcast_to(load[0:1, k * W : (k + 1) * W], (8, W))
        tile = jnp.where(side == 0, row, unit)
        vec_out[8 * k : 8 * k + 8, :] = tile
        split[k] = split_rows(tile)
        vec.append(tile)
    for level in range(LEVELS):
        copies[level].wait()
        for j in range(NB):
            store_split(raw[level * NB + j], coupling, level * NB + j)
        for j in range(NB):
            put(payload, level, j, times_t(split[sep[level, j]], coupling[level * NB + j]))
    factor_copy.wait()
    shunt_copy.wait()
    for k in range(NB):
        store_split(raw_factor[k], factor, k)
    payload[LEVELS * ROWS :, :] = local_square(vec, pre_diag(shunt), 0.25, factor, inner_out)


def make_early_kernel(precond):
    def kernel(sum0, sum1, vec, inner, shunt, factor, coupling, place, acc):
        weights = PRE if precond else OP
        diag = pre_diag(shunt) if precond else own_diag(shunt)
        scale = 0.25 if precond else 1.0
        tiles = [
            diag[k] * tile_of(vec, k) + scale * times_t(inner[k], factor[k]) for k in range(NB)
        ]
        back = coarse_back(0, sum0, weights, coupling, place)
        back = back + coarse_back(1, sum1, weights, coupling, place)
        acc[...] = back + jnp.concatenate(tiles, axis=0)

    return kernel


def make_middle_kernel(precond):
    def kernel(sum2, early, coupling, place, acc):
        weights = PRE if precond else OP
        acc[...] = early[...] + coarse_back(2, sum2, weights, coupling, place)

    return kernel


def make_precond_kernel(first):
    def kernel(sum3, sum4, square, middle, shunt, factor, coupling, flipped, pick, place, *refs):
        if not first:
            old_direction, old_rho = refs[:2]
            refs = refs[2:]
        payload, inner, direction, rho = refs
        acc = middle[...] + coarse_back(3, sum3, PRE, coupling, place)
        acc = acc + coarse_back(4, sum4, PRE, coupling, place)
        rho_new = side_totals(square)
        if not first:
            ratio = rho_new / old_rho[...]
        rho[...] = rho_new
        vec = []
        for k in range(NB):
            tile = acc[8 * k : 8 * k + 8]
            if not first:
                tile = tile + ratio * tile_of(old_direction, k)
            tile = keep_sides(tile)
            direction[8 * k : 8 * k + 8, :] = tile
            vec.append(tile)
        contributions(vec, flipped, pick, payload)
        payload[LEVELS * ROWS :, :] = local_square(vec, own_diag(shunt), 1.0, factor, inner)

    return kernel


def make_operator_kernel(first):
    def kernel(sum3, sum4, square, middle, shunt, factor, coupling, flipped, pick, place, *refs):
        direction, residual, rho = refs[:3]
        refs = refs[3:]
        if not first:
            estimate = refs[0]
            refs = refs[1:]
        payload, inner, next_residual, next_estimate = refs
        acc = middle[...] + coarse_back(3, sum3, OP, coupling, place)
        acc = acc + coarse_back(4, sum4, OP, coupling, place)
        step = rho[...] / side_totals(square)
        vec = []
        for k in range(NB):
            tile = keep_sides(tile_of(residual, k) - step * acc[8 * k : 8 * k + 8])
            next_residual[8 * k : 8 * k + 8, :] = tile
            vec.append(tile)
        contributions(vec, flipped, pick, payload)
        payload[LEVELS * ROWS :, :] = local_square(vec, pre_diag(shunt), 0.25, factor, inner)
        for k in range(NB):
            gain = step * tile_of(direction, k)
            next_estimate[8 * k : 8 * k + 8, :] = gain if first else tile_of(estimate, k) + gain

    return kernel


def drops_kernel(vec, ends, drops):
    def chunk(i, carry):
        here = pl.ds(pl.multiple_of(8 * i, 8), 8)

        def at(end):
            index = ends[end, here, :]
            block = index >> 7
            lane = index & (W - 1)
            values = [jnp.zeros((8, W), F32)] * 2
            for k in range(NB):
                chosen = block == k
                for side in range(2):
                    row = jnp.broadcast_to(vec[8 * k + side : 8 * k + side + 1, :], (8, W))
                    found = jnp.take_along_axis(row, lane, axis=1)
                    values[side] = jnp.where(chosen, found, values[side])
            return values

        low, high = at(0), at(1)
        for side in range(2):
            drops[side, here, :] = low[side] - high[side]
        return carry

    lax.fori_loop(0, drops.shape[1] // 8, chunk, 0)


def last_kernel(square, direction, rho, estimate, known, change, volts, terms):
    step = rho[...] / side_totals(square)
    for side in range(2):
        gain = jnp.broadcast_to(step[side : side + 1, :], (8, W))
        if side == 0:
            forward = gain
        else:
            adjoint = gain
    for i in range(terms.shape[0] // 8):
        here = slice(8 * i, 8 * i + 8)
        drop = known[0, here, :] + forward * change[0, here, :]
        back = known[1, here, :] + adjoint * change[1, here, :]
        terms[here, :] = -(back * drop)
    for k in range(NB):
        tile = tile_of(estimate, k) + step * tile_of(direction, k)
        volts[0, k : k + 1, :] = tile[0:1]
        volts[1, k : k + 1, :] = tile[1:2]


TILES = jax.ShapeDtypeStruct((FLAT, W), F32)
PAYLOAD = jax.ShapeDtypeStruct((LEVELS * ROWS + 8, W), F32)
TILE = jax.ShapeDtypeStruct((8, W), F32)
INNER = jax.ShapeDtypeStruct((NB, 16, W), BF16)
COUPLING = jax.ShapeDtypeStruct((LEVELS * NB, 2 * W, W), BF16)
FACTOR = jax.ShapeDtypeStruct((NB, 2 * W, W), BF16)
PICK = jax.ShapeDtypeStruct((16 * LEVELS * NB, 256), BF16)
PLACE = jax.ShapeDtypeStruct((LEVELS, FLAT, 256), BF16)


def call(kernel, name, args, outs, scratch=(), smem=0, hbm=(), limit=16):
    specs = [SMEM if i < smem else HBM if i in hbm else VMEM for i in range(len(args))]
    one = not isinstance(outs, list)
    return pl.pallas_call(
        kernel,
        in_specs=specs,
        out_specs=VMEM if one else [VMEM] * len(outs),
        out_shape=outs,
        scratch_shapes=list(scratch),
        compiler_params=pltpu.CompilerParams(vmem_limit_bytes=limit * MIB),
        name=name,
    )(*args)


OTHER_QUAD = {0: 6, 1: 7, 2: 4, 3: 5, 4: 2, 5: 3, 6: 0, 7: 1}


def partners(kind, count):
    if kind == "other":
        return [(s, s // 8 * 8 + OTHER_QUAD[s % 8]) for s in range(count)]
    return [(s, s ^ kind) for s in range(count)]


def power(rows):
    return rows[:8] * rows[:8] + rows[8:16] * rows[8:16] + rows[16:] * rows[16:]


def tree_exchange(payload, weights, jobs):
    count = lax.axis_size("dom")

    def fetch(value, kinds, number, finished, results):
        got = [lax.ppermute(value, "dom", partners(kind, count)) for kind in kinds]
        if number in jobs:
            results[number] = jobs[number](finished, results)
            got, results[number] = lax.optimization_barrier((got, results[number]))
        return got

    def quad(value, kinds, number, finished, results, level):
        near, far, farther = fetch(value, kinds, number, finished, results)
        pair = value[:-8] + near[:-8]
        other = far[:-8] + farther[:-8]
        low = pair[:ROWS]
        both = pair[ROWS:] + other[ROWS:]
        high = both[:ROWS]
        square = (value[-8:] + near[-8:]) + (far[-8:] + farther[-8:])
        square = square + weights[level] * (power(low) + power(other[:ROWS]))
        square = square + weights[level + 1] * power(high)
        return low, high, both[ROWS:], square

    results = {}
    low, high, pending, square = quad(payload, (1, 2, 3), 0, [], results, 0)
    finished = [low, high]
    pending = jnp.concatenate([pending, square], axis=0)
    (received,) = fetch(pending, ("other",), 1, finished, results)
    total = pending + received
    finished.append(total[:ROWS])
    square = total[-8:] + weights[2] * power(total[:ROWS])
    pending = jnp.concatenate([total[ROWS:-8], square], axis=0)
    low, high, _, square = quad(pending, (8, 16, 24), 2, finished, results, 3)
    return low, high, square, results


def shards(
    load_current, worst_node, cond_diag, branch, precond_factor, coupling, sep_map, strap_ends
):
    node_count = NB * W
    shunt = cond_diag.reshape(NB, W)
    target = worst_node - lax.axis_index("dom") * node_count
    ends = strap_ends.reshape(2, -1, W)
    strap_rows = ends.shape[1]
    drops_shape = jax.ShapeDtypeStruct(ends.shape, F32)

    payload, inner, residual, cpl, pre, pick, place = call(
        first_kernel,
        "first_part",
        (
            sep_map,
            target,
            pltpu.with_memory_space_constraint(load_current, pltpu.HBM),
            pltpu.with_memory_space_constraint(shunt, pltpu.HBM),
            pltpu.with_memory_space_constraint(coupling.reshape(LEVELS * NB, W, W), pltpu.HBM),
            pltpu.with_memory_space_constraint(precond_factor, pltpu.HBM),
        ),
        [PAYLOAD, INNER, TILES, COUPLING, FACTOR, PICK, PLACE],
        [
            pltpu.VMEM((1, node_count), F32),
            pltpu.VMEM((NB, W), F32),
            pltpu.VMEM((LEVELS * NB, W, W), F32),
            pltpu.VMEM((NB, W, W), F32),
            pltpu.VMEM((NB, 16, W), BF16),
            pltpu.SemaphoreType.DMA((LEVELS + 3,)),
        ],
        smem=2,
        hbm=(2, 3, 4, 5),
        limit=24,
    )
    direction = rho = estimate = flipped = brn = None

    def exchange(payload, precond, vec, inner, factor, jobs, back=True):
        def early(finished, results):
            args = (finished[0], finished[1], vec, inner, shunt, factor, cpl, place)
            return call(make_early_kernel(precond), "early_levels", args, TILES)

        def middle(finished, results):
            args = (finished[2], results[1], cpl, place)
            return call(make_middle_kernel(precond), "middle_level", args, TILES)

        if back:
            jobs = {**jobs, 1: early, 2: middle}
        return tree_exchange(payload, PRE if precond else OP, jobs)

    for iteration in range(ITERS):
        first = iteration == 0
        last = iteration + 1 == ITERS
        jobs = {}
        if first:
            jobs[0] = lambda *_: (
                call(split_kernel, "split_branch", (branch,), FACTOR),
                call(transpose_kernel, "flip", (cpl,), COUPLING),
            )
        if last:
            jobs[0] = lambda *_: call(drops_kernel, "known", (estimate, ends), drops_shape)
        sum3, sum4, square, results = exchange(payload, True, residual, inner, pre, jobs)
        if first:
            brn, flipped = results[0]
        if last:
            known = results[0]
        args = (sum3, sum4, square, results[2], shunt, brn, cpl, flipped, pick, place)
        if not first:
            args += (direction, rho)
        payload, inner, direction, rho = call(
            make_precond_kernel(first), "precond_round", args, [PAYLOAD, INNER, TILES, TILE]
        )
        jobs = {}
        if last:
            jobs[0] = lambda *_: call(drops_kernel, "change", (direction, ends), drops_shape)
        sum3, sum4, square, results = exchange(
            payload, False, direction, inner, brn, jobs, not last
        )
        if last:
            change = results[0]
        else:
            args = (sum3, sum4, square, results[2], shunt, pre, cpl, flipped, pick, place)
            args += (direction, residual, rho)
            if not first:
                args += (estimate,)
            payload, inner, residual, estimate = call(
                make_operator_kernel(first), "operator_round", args, [PAYLOAD, INNER, TILES, TILES]
            )
    volts, terms = call(
        last_kernel,
        "straps",
        (square, direction, rho, estimate, known, change),
        [
            jax.ShapeDtypeStruct((2, NB, W), F32),
            jax.ShapeDtypeStruct((strap_rows, W), F32),
        ],
    )
    terms = terms + lax.ppermute(terms, "load", [(s, s ^ 1) for s in range(8)])
    near, far, farther = [
        lax.ppermute(terms, "load", [(s, s ^ mask) for s in range(8)]) for mask in (2, 4, 6)
    ]
    terms = (terms + near) + (far + farther)
    return (volts.reshape(2, 1, node_count), terms.reshape(-1))


def solution(mesh):
    placed = (
        P("load", "dom"),
        P("load"),
        P("dom"),
        P("dom", None, None),
        P("dom", None, None),
        P(None, "dom", None, None),
        P(None, "dom"),
        P(None, "dom"),
    )
    return jax.shard_map(
        shards,
        mesh=mesh,
        in_specs=placed,
        out_specs=(P(None, "load", "dom"), P("dom")),
        check_vma=False,
    )
```

```python
import math

import jax
import jax.numpy as jnp
from jax import lax
from jax.experimental import pallas as pl
from jax.experimental.pallas import tpu as pltpu
from jax.sharding import PartitionSpec as P

ITERS = 4
LEVELS = 5
NB = 12
W = 128
ROWS = 2 * NB
FLAT = 8 * NB
OP = [1.0 / math.sqrt(2.0 ** (level + 1)) for level in range(LEVELS)]
PRE = [0.5 * c for c in OP]
F32 = jnp.float32
BF16 = jnp.bfloat16
VMEM = pl.BlockSpec(memory_space=pltpu.VMEM)
SMEM = pl.BlockSpec(memory_space=pltpu.SMEM)
HBM = pl.BlockSpec(memory_space=pltpu.HBM)
MIB = 1024 * 1024


def split_rows(tile):
    high = tile.astype(BF16).astype(F32)
    return jnp.concatenate([high, tile - high], axis=0).astype(BF16)


def times(rows, matrix):
    out = lax.dot_general(
        jnp.concatenate([rows, rows], axis=1),
        matrix,
        (((1,), (0,)), ((), ())),
        preferred_element_type=F32,
    )
    return out[:8] + out[8:]


def times_t(rows, matrix):
    out = lax.dot_general(rows, matrix, (((1,), (1,)), ((), ())), preferred_element_type=F32)
    out = out[:8] + out[8:]
    return out[:, :W] + out[:, W:]


def store_split(mats, out, index):
    high = mats.astype(BF16)
    out[index, :W, :] = high
    out[index, W:, :] = (mats - high.astype(F32)).astype(BF16)


def split_kernel(mat_ref, out_ref):
    for j in range(NB):
        store_split(mat_ref[j], out_ref, j)


def transpose_kernel(coupling, flipped):
    row = lax.broadcasted_iota(jnp.int32, (W, W), 0)
    eye = (row == lax.broadcasted_iota(jnp.int32, (W, W), 1)).astype(F32).astype(BF16)
    for i in range(LEVELS * NB):
        out = lax.dot_general(
            eye, coupling[i], (((1,), (1,)), ((), ())), preferred_element_type=F32
        ).astype(BF16)
        flipped[i, :W, :] = out[:, :W]
        flipped[i, W:, :] = out[:, W:]


def side_totals(square):
    total = square[...]
    total = total + pltpu.roll(total, 2, 0)
    total = total + pltpu.roll(total, 4, 0)
    return jnp.broadcast_to(jnp.sum(total, axis=1, keepdims=True), (8, W))


def keep_sides(tile):
    return jnp.where(lax.broadcasted_iota(jnp.int32, (8, W), 0) < 2, tile, 0.0)


def tile_of(ref, k):
    return ref[8 * k : 8 * k + 8, :]


def stacked(values):
    high = values.astype(BF16).astype(F32)
    parts = [high, values - high]
    spare = -2 * values.shape[0] % W
    if spare:
        parts.append(jnp.zeros((spare, W), F32))
    return jnp.concatenate(parts, axis=0).astype(BF16)


def dot(left, right):
    return lax.dot_general(left, right, (((1,), (0,)), ((), ())), preferred_element_type=F32)


def place_matrix(sep, levels):
    used = FLAT * len(levels)
    width = 2 * used + -2 * used % W
    row = lax.broadcasted_iota(jnp.int32, (8, width), 0)
    col = lax.broadcasted_iota(jnp.int32, (8, width), 1)
    inside = jnp.where(col >= used, col - used, col)
    number = jnp.where(inside >= FLAT, 1, 0)
    inside = inside - FLAT * number
    block = inside >> 3
    valid = (row < 2) & (col < 2 * used) & ((inside & 7) == 2 * (block & 3) + row)
    owner = jnp.full((8, width), -1, jnp.int32)
    for n, level in enumerate(levels):
        for j in range(NB):
            owner = jnp.where(valid & (number == n) & (block == j), sep[level, j], owner)
    tiles = [jnp.where(owner == k, 1.0, 0.0) for k in range(NB)]
    return jnp.concatenate(tiles, axis=0).astype(BF16)


def coarse_back(levels, totals, weights, coupling, place):
    outs = []
    for level, total in zip(levels, totals):
        for group in range(NB // 4):
            rows = split_rows(total[8 * group : 8 * group + 8, :] * weights[level])
            for member in range(4):
                outs.append(times(rows, coupling[level * NB + 4 * group + member]))
    return dot(place[...], stacked(jnp.concatenate(outs, axis=0)))


def local_square(vec, diag, scale, factor, inner_out):
    square = jnp.zeros((8, W), F32)
    for k in range(NB):
        inner = times(split_rows(vec[k]), factor[k])
        if inner_out is not None:
            inner_out[k] = split_rows(inner)
        square = square + (diag[k] * vec[k] * vec[k] + scale * (inner * inner))
    return square


def put(payload, level, j, out):
    payload[level * ROWS + 2 * j : level * ROWS + 2 * j + 2, :] = out[0:2]


def contributions(flipped, sep, split, payload):
    for level in range(LEVELS):
        for j in range(NB):
            put(payload, level, j, times(split[sep[level, j]], flipped[level * NB + j]))


def own_diag(shunt):
    return [jnp.broadcast_to(shunt[k : k + 1, :], (8, W)) for k in range(NB)]


def pre_diag(shunt):
    return [1.0 / (tile + 1.0) for tile in own_diag(shunt)]


def first_kernel(
    sep,
    target,
    load_hbm,
    shunt_hbm,
    coupling_hbm,
    factor_hbm,
    payload,
    inner_out,
    vec_out,
    coupling,
    factor,
    place01,
    place2,
    place34,
    load,
    shunt,
    raw,
    raw_factor,
    split,
    sems,
):
    copies = [
        pltpu.make_async_copy(
            coupling_hbm.at[pl.ds(level * NB, NB)], raw.at[pl.ds(level * NB, NB)], sems.at[level]
        )
        for level in range(LEVELS)
    ]
    factor_copy = pltpu.make_async_copy(factor_hbm, raw_factor, sems.at[LEVELS])
    load_copy = pltpu.make_async_copy(load_hbm, load, sems.at[LEVELS + 1])
    shunt_copy = pltpu.make_async_copy(shunt_hbm, shunt, sems.at[LEVELS + 2])
    load_copy.start()
    shunt_copy.start()
    for copy in copies:
        copy.start()
    factor_copy.start()
    place01[...] = place_matrix(sep, (0, 1))
    place2[...] = place_matrix(sep, (2,))
    place34[...] = place_matrix(sep, (3, 4))
    load_copy.wait()
    side = lax.broadcasted_iota(jnp.int32, (8, W), 0)
    lane = lax.broadcasted_iota(jnp.int32, (8, W), 1)
    vec = []
    for k in range(NB):
        unit = jnp.where((side == 1) & (lane + k * W == target[0]), 1.0, 0.0)
        row = jnp.broadcast_to(load[0:1, k * W : (k + 1) * W], (8, W))
        tile = jnp.where(side == 0, row, unit)
        vec_out[8 * k : 8 * k + 8, :] = tile
        split[k] = split_rows(tile)
        vec.append(tile)
    for level in range(LEVELS):
        copies[level].wait()
        for j in range(NB):
            store_split(raw[level * NB + j], coupling, level * NB + j)
        for j in range(NB):
            put(payload, level, j, times_t(split[sep[level, j]], coupling[level * NB + j]))
    factor_copy.wait()
    shunt_copy.wait()
    for k in range(NB):
        store_split(raw_factor[k], factor, k)
    payload[LEVELS * ROWS :, :] = local_square(vec, pre_diag(shunt), 0.25, factor, inner_out)


def make_early_kernel(precond):
    def kernel(sum0, sum1, vec, inner, shunt, factor, coupling, place, acc):
        weights = PRE if precond else OP
        diag = pre_diag(shunt) if precond else own_diag(shunt)
        scale = 0.25 if precond else 1.0
        tiles = [
            diag[k] * tile_of(vec, k) + scale * times_t(inner[k], factor[k]) for k in range(NB)
        ]
        back = coarse_back((0, 1), (sum0, sum1), weights, coupling, place)
        acc[...] = back + jnp.concatenate(tiles, axis=0)

    return kernel


def make_middle_kernel(precond):
    def kernel(sum2, early, coupling, place, acc):
        weights = PRE if precond else OP
        acc[...] = early[...] + coarse_back((2,), (sum2,), weights, coupling, place)

    return kernel


def make_precond_kernel(first, last):
    def kernel(sep_vmem, sum3, sum4, square, middle, shunt, factor, coupling, flipped, place, *refs):
        if not first:
            old_direction, old_rho = refs[:2]
            refs = refs[2:]
        inner = None
        if not last:
            inner = refs[0]
            refs = refs[1:]
        payload, direction, rho, sep, split, sem = refs
        copy = pltpu.make_async_copy(sep_vmem, sep, sem)
        copy.start()
        acc = middle[...] + coarse_back((3, 4), (sum3, sum4), PRE, coupling, place)
        rho_new = side_totals(square)
        if not first:
            ratio = rho_new / old_rho[...]
        rho[...] = rho_new
        vec = []
        for k in range(NB):
            tile = acc[8 * k : 8 * k + 8]
            if not first:
                tile = tile + ratio * tile_of(old_direction, k)
            tile = keep_sides(tile)
            direction[8 * k : 8 * k + 8, :] = tile
            split[k] = split_rows(tile)
            vec.append(tile)
        copy.wait()
        contributions(flipped, sep, split, payload)
        payload[LEVELS * ROWS :, :] = local_square(vec, own_diag(shunt), 1.0, factor, inner)

    return kernel


def make_operator_kernel(first):
    def kernel(sep_vmem, sum3, sum4, square, middle, shunt, factor, coupling, flipped, place, *refs):
        direction, residual, rho = refs[:3]
        refs = refs[3:]
        if not first:
            estimate = refs[0]
            refs = refs[1:]
        inner, payload, next_residual, next_estimate, sep, split, sem = refs
        copy = pltpu.make_async_copy(sep_vmem, sep, sem)
        copy.start()
        acc = middle[...] + coarse_back((3, 4), (sum3, sum4), OP, coupling, place)
        step = rho[...] / side_totals(square)
        vec = []
        for k in range(NB):
            tile = keep_sides(tile_of(residual, k) - step * acc[8 * k : 8 * k + 8])
            next_residual[8 * k : 8 * k + 8, :] = tile
            split[k] = split_rows(tile)
            vec.append(tile)
        copy.wait()
        contributions(flipped, sep, split, payload)
        payload[LEVELS * ROWS :, :] = local_square(vec, pre_diag(shunt), 0.25, factor, inner)
        for k in range(NB):
            gain = step * tile_of(direction, k)
            next_estimate[8 * k : 8 * k + 8, :] = gain if first else tile_of(estimate, k) + gain

    return kernel


def drops_kernel(vec, ends, drops):
    def chunk(i, carry):
        here = pl.ds(pl.multiple_of(8 * i, 8), 8)

        def at(end):
            index = ends[end, here, :]
            block = index >> 7
            lane = index & (W - 1)
            values = [jnp.zeros((8, W), F32)] * 2
            for k in range(NB):
                chosen = block == k
                for side in range(2):
                    row = jnp.broadcast_to(vec[8 * k + side : 8 * k + side + 1, :], (8, W))
                    found = jnp.take_along_axis(row, lane, axis=1)
                    values[side] = jnp.where(chosen, found, values[side])
            return values

        low, high = at(0), at(1)
        for side in range(2):
            drops[side, here, :] = low[side] - high[side]
        return carry

    lax.fori_loop(0, drops.shape[1] // 8, chunk, 0)


def last_kernel(square, direction, rho, estimate, known, change, volts, terms):
    step = rho[...] / side_totals(square)
    for side in range(2):
        gain = jnp.broadcast_to(step[side : side + 1, :], (8, W))
        if side == 0:
            forward = gain
        else:
            adjoint = gain
    for i in range(terms.shape[0] // 8):
        here = slice(8 * i, 8 * i + 8)
        drop = known[0, here, :] + forward * change[0, here, :]
        back = known[1, here, :] + adjoint * change[1, here, :]
        terms[here, :] = -(back * drop)
    for k in range(NB):
        tile = tile_of(estimate, k) + step * tile_of(direction, k)
        volts[0, k : k + 1, :] = tile[0:1]
        volts[1, k : k + 1, :] = tile[1:2]


TILES = jax.ShapeDtypeStruct((FLAT, W), F32)
PAYLOAD = jax.ShapeDtypeStruct((LEVELS * ROWS + 8, W), F32)
TILE = jax.ShapeDtypeStruct((8, W), F32)
INNER = jax.ShapeDtypeStruct((NB, 16, W), BF16)
COUPLING = jax.ShapeDtypeStruct((LEVELS * NB, 2 * W, W), BF16)
FACTOR = jax.ShapeDtypeStruct((NB, 2 * W, W), BF16)
PLACE = jax.ShapeDtypeStruct((FLAT, 256), BF16)
PLACE_TWO = jax.ShapeDtypeStruct((FLAT, 4 * FLAT), BF16)
SEP_SCRATCH = [
    pltpu.SMEM((LEVELS, NB), jnp.int32),
    pltpu.VMEM((NB, 16, W), BF16),
    pltpu.SemaphoreType.DMA,
]


def call(kernel, name, args, outs, scratch=(), smem=0, hbm=(), limit=16):
    specs = [SMEM if i < smem else HBM if i in hbm else VMEM for i in range(len(args))]
    one = not isinstance(outs, list)
    return pl.pallas_call(
        kernel,
        in_specs=specs,
        out_specs=VMEM if one else [VMEM] * len(outs),
        out_shape=outs,
        scratch_shapes=list(scratch),
        compiler_params=pltpu.CompilerParams(vmem_limit_bytes=limit * MIB),
        name=name,
    )(*args)


OTHER_QUAD = {0: 6, 1: 7, 2: 4, 3: 5, 4: 2, 5: 3, 6: 0, 7: 1}


def partners(kind, count):
    if kind == "other":
        return [(s, s // 8 * 8 + OTHER_QUAD[s % 8]) for s in range(count)]
    return [(s, s ^ kind) for s in range(count)]


def power(rows):
    return rows[:8] * rows[:8] + rows[8:16] * rows[8:16] + rows[16:] * rows[16:]


def tree_exchange(payload, weights, jobs):
    count = lax.axis_size("dom")

    def fetch(value, kinds, number, finished, results):
        got = [lax.ppermute(value, "dom", partners(kind, count)) for kind in kinds]
        if number in jobs:
            results[number] = jobs[number](finished, results)
            got, results[number] = lax.optimization_barrier((got, results[number]))
            return got
        return lax.optimization_barrier(got)

    def quad(value, kinds, number, finished, results, level):
        farther, far, near = fetch(value, kinds, number, finished, results)
        pair = value[:-8] + near[:-8]
        other = far[:-8] + farther[:-8]
        low = pair[:ROWS]
        both = pair[ROWS:] + other[ROWS:]
        high = both[:ROWS]
        square = (value[-8:] + near[-8:]) + (far[-8:] + farther[-8:])
        square = square + weights[level] * (power(low) + power(other[:ROWS]))
        square = square + weights[level + 1] * power(high)
        return low, high, both[ROWS:], square

    results = {}
    low, high, pending, square = quad(payload, (3, 2, 1), 0, [], results, 0)
    finished = [low, high]
    pending = jnp.concatenate([pending, square], axis=0)
    (received,) = fetch(pending, ("other",), 1, finished, results)
    total = pending + received
    finished.append(total[:ROWS])
    square = total[-8:] + weights[2] * power(total[:ROWS])
    pending = jnp.concatenate([total[ROWS:-8], square], axis=0)
    low, high, _, square = quad(pending, (24, 16, 8), 2, finished, results, 3)
    return low, high, square, results


def shards(
    load_current, worst_node, cond_diag, branch, precond_factor, coupling, sep_map, strap_ends
):
    node_count = NB * W
    shunt = cond_diag.reshape(NB, W)
    target = worst_node - lax.axis_index("dom") * node_count
    ends = strap_ends.reshape(2, -1, W)
    strap_rows = ends.shape[1]
    drops_shape = jax.ShapeDtypeStruct(ends.shape, F32)

    payload, inner, residual, cpl, pre, place01, place2, place34 = call(
        first_kernel,
        "first_part",
        (
            sep_map,
            target,
            pltpu.with_memory_space_constraint(load_current, pltpu.HBM),
            pltpu.with_memory_space_constraint(shunt, pltpu.HBM),
            pltpu.with_memory_space_constraint(coupling.reshape(LEVELS * NB, W, W), pltpu.HBM),
            pltpu.with_memory_space_constraint(precond_factor, pltpu.HBM),
        ),
        [PAYLOAD, INNER, TILES, COUPLING, FACTOR, PLACE_TWO, PLACE, PLACE_TWO],
        [
            pltpu.VMEM((1, node_count), F32),
            pltpu.VMEM((NB, W), F32),
            pltpu.VMEM((LEVELS * NB, W, W), F32),
            pltpu.VMEM((NB, W, W), F32),
            pltpu.VMEM((NB, 16, W), BF16),
            pltpu.SemaphoreType.DMA((LEVELS + 3,)),
        ],
        smem=2,
        hbm=(2, 3, 4, 5),
        limit=24,
    )
    direction = rho = estimate = flipped = brn = None

    def exchange(payload, precond, vec, inner, factor, jobs, back=True):
        def early(finished, results):
            args = (finished[0], finished[1], vec, inner, shunt, factor, cpl, place01)
            return call(make_early_kernel(precond), "early_levels", args, TILES)

        def middle(finished, results):
            args = (finished[2], results[1], cpl, place2)
            return call(make_middle_kernel(precond), "middle_level", args, TILES)

        if back:
            jobs = {**jobs, 1: early, 2: middle}
        return tree_exchange(payload, PRE if precond else OP, jobs)

    for iteration in range(ITERS):
        first = iteration == 0
        last = iteration + 1 == ITERS
        jobs = {}
        if first:
            jobs[0] = lambda *_: (
                call(split_kernel, "split_branch", (branch,), FACTOR),
                call(transpose_kernel, "flip", (cpl,), COUPLING),
            )
        if last:
            jobs[0] = lambda *_: call(drops_kernel, "known", (estimate, ends), drops_shape)
        sum3, sum4, square, results = exchange(payload, True, residual, inner, pre, jobs)
        if first:
            brn, flipped = results[0]
        if last:
            known = results[0]
        args = (sep_map, sum3, sum4, square, results[2], shunt, brn, cpl, flipped, place34)
        if not first:
            args += (direction, rho)
        outs = [PAYLOAD, TILES, TILE]
        *inner, payload, direction, rho = call(
            make_precond_kernel(first, last),
            "precond_round",
            args,
            outs if last else [INNER] + outs,
            SEP_SCRATCH,
        )
        inner = None if last else inner[0]
        jobs = {}
        if last:
            jobs[0] = lambda *_: call(drops_kernel, "change", (direction, ends), drops_shape)
        sum3, sum4, square, results = exchange(
            payload, False, direction, inner, brn, jobs, not last
        )
        if last:
            change = results[0]
        else:
            args = (sep_map, sum3, sum4, square, results[2], shunt, pre, cpl, flipped, place34)
            args += (direction, residual, rho)
            if not first:
                args += (estimate,)
            inner, payload, residual, estimate = call(
                make_operator_kernel(first),
                "operator_round",
                args,
                [INNER, PAYLOAD, TILES, TILES],
                SEP_SCRATCH,
            )
    volts, terms = call(
        last_kernel,
        "straps",
        (square, direction, rho, estimate, known, change),
        [
            jax.ShapeDtypeStruct((2, NB, W), F32),
            jax.ShapeDtypeStruct((strap_rows, W), F32),
        ],
    )
    terms = terms + lax.ppermute(terms, "load", [(s, s ^ 1) for s in range(8)])
    near, far, farther = [
        lax.ppermute(terms, "load", [(s, s ^ mask) for s in range(8)]) for mask in (2, 4, 6)
    ]
    terms = (terms + near) + (far + farther)
    return (volts.reshape(2, 1, node_count), terms.reshape(-1))


def solution(mesh):
    placed = (
        P("load", "dom"),
        P("load"),
        P("dom"),
        P("dom", None, None),
        P("dom", None, None),
        P(None, "dom", None, None),
        P(None, "dom"),
        P(None, "dom"),
    )
    return jax.shard_map(
        shards,
        mesh=mesh,
        in_specs=placed,
        out_specs=(P(None, "load", "dom"), P("dom")),
        check_vma=False,
    )
```

```python
import math

import jax
import jax.numpy as jnp
from jax import lax
from jax.experimental import pallas as pl
from jax.experimental.pallas import tpu as pltpu
from jax.sharding import PartitionSpec as P

ITERS = 4
LEVELS = 5
NB = 12
W = 128
ROWS = 2 * NB
FLAT = 8 * NB
CHUNK = 6
OP = [1.0 / math.sqrt(2.0 ** (level + 1)) for level in range(LEVELS)]
PRE = [0.5 * c for c in OP]
F32 = jnp.float32
BF16 = jnp.bfloat16
VMEM = pl.BlockSpec(memory_space=pltpu.VMEM)
SMEM = pl.BlockSpec(memory_space=pltpu.SMEM)
HBM = pl.BlockSpec(memory_space=pltpu.HBM)
MIB = 1024 * 1024


def split_rows(tile):
    high = tile.astype(BF16).astype(F32)
    return jnp.concatenate([high, tile - high], axis=0).astype(BF16)


def times(rows, matrix):
    out = lax.dot_general(
        jnp.concatenate([rows, rows], axis=1),
        matrix,
        (((1,), (0,)), ((), ())),
        preferred_element_type=F32,
    )
    return out[:8] + out[8:]


def times_t(rows, matrix):
    out = lax.dot_general(rows, matrix, (((1,), (1,)), ((), ())), preferred_element_type=F32)
    out = out[:8] + out[8:]
    return out[:, :W] + out[:, W:]


def store_split(mats, out, index):
    high = mats.astype(BF16)
    out[index, :W, :] = high
    out[index, W:, :] = (mats - high.astype(F32)).astype(BF16)


def split_kernel(mat_ref, out_ref):
    for j in range(NB):
        store_split(mat_ref[j], out_ref, j)


def transpose_kernel(coupling, flipped):
    row = lax.broadcasted_iota(jnp.int32, (W, W), 0)
    eye = (row == lax.broadcasted_iota(jnp.int32, (W, W), 1)).astype(F32).astype(BF16)
    for i in range(LEVELS * NB):
        out = lax.dot_general(
            eye, coupling[i], (((1,), (1,)), ((), ())), preferred_element_type=F32
        ).astype(BF16)
        flipped[i, :W, :] = out[:, :W]
        flipped[i, W:, :] = out[:, W:]


def side_totals(square):
    total = square[...]
    total = total + pltpu.roll(total, 2, 0)
    total = total + pltpu.roll(total, 4, 0)
    return jnp.broadcast_to(jnp.sum(total, axis=1, keepdims=True), (8, W))


def keep_sides(tile):
    return jnp.where(lax.broadcasted_iota(jnp.int32, (8, W), 0) < 2, tile, 0.0)


def tile_of(ref, k):
    return ref[8 * k : 8 * k + 8, :]


def stacked(values):
    high = values.astype(BF16).astype(F32)
    parts = [high, values - high]
    spare = -2 * values.shape[0] % W
    if spare:
        parts.append(jnp.zeros((spare, W), F32))
    return jnp.concatenate(parts, axis=0).astype(BF16)


def dot(left, right):
    return lax.dot_general(left, right, (((1,), (0,)), ((), ())), preferred_element_type=F32)


def place_matrix(sep, levels):
    used = FLAT * len(levels)
    width = 2 * used + -2 * used % W
    row = lax.broadcasted_iota(jnp.int32, (8, width), 0)
    col = lax.broadcasted_iota(jnp.int32, (8, width), 1)
    inside = jnp.where(col >= used, col - used, col)
    number = jnp.where(inside >= FLAT, 1, 0)
    inside = inside - FLAT * number
    block = inside >> 3
    valid = (row < 2) & (col < 2 * used) & ((inside & 7) == 2 * (block & 3) + row)
    owner = jnp.full((8, width), -1, jnp.int32)
    for n, level in enumerate(levels):
        for j in range(NB):
            owner = jnp.where(valid & (number == n) & (block == j), sep[level, j], owner)
    tiles = [jnp.where(owner == k, 1.0, 0.0) for k in range(NB)]
    return jnp.concatenate(tiles, axis=0).astype(BF16)


def coarse_back(levels, totals, weights, coupling, place):
    outs = []
    for level, total in zip(levels, totals):
        for group in range(NB // 4):
            rows = split_rows(total[8 * group : 8 * group + 8, :] * weights[level])
            for member in range(4):
                outs.append(times(rows, coupling[level * NB + 4 * group + member]))
    return dot(place[...], stacked(jnp.concatenate(outs, axis=0)))


def local_square(vec, diag, scale, factor, inner_out):
    square = jnp.zeros((8, W), F32)
    for k in range(NB):
        inner = times(split_rows(vec[k]), factor[k])
        if inner_out is not None:
            inner_out[k] = split_rows(inner)
        square = square + (diag[k] * vec[k] * vec[k] + scale * (inner * inner))
    return square


def put(payload, level, j, out):
    payload[level * ROWS + 2 * j : level * ROWS + 2 * j + 2, :] = out[0:2]


def contributions(flipped, sep, split, payload):
    for level in range(LEVELS):
        for j in range(NB):
            put(payload, level, j, times(split[sep[level, j]], flipped[level * NB + j]))


def own_diag(shunt):
    return [jnp.broadcast_to(shunt[k : k + 1, :], (8, W)) for k in range(NB)]


def pre_diag(shunt):
    return [1.0 / (tile + 1.0) for tile in own_diag(shunt)]


def first_kernel(
    sep_hbm,
    target,
    load_hbm,
    shunt_hbm,
    coupling_hbm,
    factor_hbm,
    payload,
    inner_out,
    vec_out,
    coupling,
    factor,
    place01,
    place2,
    place34,
    sep,
    load,
    shunt,
    raw,
    raw_factor,
    split,
    small_sems,
    sems,
):
    small = [
        pltpu.make_async_copy(source, place, small_sems.at[n])
        for n, (source, place) in enumerate(
            ((sep_hbm, sep), (load_hbm, load), (shunt_hbm, shunt), (factor_hbm, raw_factor))
        )
    ]
    copies = [
        pltpu.make_async_copy(
            coupling_hbm.at[pl.ds(n * CHUNK, CHUNK)], raw.at[pl.ds(n * CHUNK, CHUNK)], sems.at[n]
        )
        for n in range(LEVELS * NB // CHUNK)
    ]
    for copy in small + copies:
        copy.start()
    small[0].wait()
    place01[...] = place_matrix(sep, (0, 1))
    place2[...] = place_matrix(sep, (2,))
    place34[...] = place_matrix(sep, (3, 4))
    small[1].wait()
    side = lax.broadcasted_iota(jnp.int32, (8, W), 0)
    lane = lax.broadcasted_iota(jnp.int32, (8, W), 1)
    goal = jnp.broadcast_to(target[...], (8, W))
    vec = []
    for k in range(NB):
        unit = jnp.where((side == 1) & (lane + k * W == goal), 1.0, 0.0)
        row = jnp.broadcast_to(load[0:1, k * W : (k + 1) * W], (8, W))
        tile = jnp.where(side == 0, row, unit)
        vec_out[8 * k : 8 * k + 8, :] = tile
        split[k] = split_rows(tile)
        vec.append(tile)
    small[2].wait()
    small[3].wait()
    for k in range(NB):
        store_split(raw_factor[k], factor, k)
    payload[LEVELS * ROWS :, :] = local_square(vec, pre_diag(shunt), 0.25, factor, inner_out)
    for n, copy in enumerate(copies):
        copy.wait()
        for i in range(n * CHUNK, (n + 1) * CHUNK):
            store_split(raw[i], coupling, i)
        for i in range(n * CHUNK, (n + 1) * CHUNK):
            level, j = divmod(i, NB)
            put(payload, level, j, times_t(split[sep[level, j]], coupling[i]))


def make_early_kernel(precond):
    def kernel(sum0, sum1, vec, inner, shunt, factor, coupling, place, acc):
        weights = PRE if precond else OP
        diag = pre_diag(shunt) if precond else own_diag(shunt)
        scale = 0.25 if precond else 1.0
        tiles = [
            diag[k] * tile_of(vec, k) + scale * times_t(inner[k], factor[k]) for k in range(NB)
        ]
        back = coarse_back((0, 1), (sum0, sum1), weights, coupling, place)
        acc[...] = back + jnp.concatenate(tiles, axis=0)

    return kernel


def make_middle_kernel(precond):
    def kernel(sum2, early, coupling, place, acc):
        weights = PRE if precond else OP
        acc[...] = early[...] + coarse_back((2,), (sum2,), weights, coupling, place)

    return kernel


def make_precond_kernel(first, last):
    def kernel(sep_vmem, sum3, sum4, square, middle, shunt, factor, coupling, flipped, place, *refs):
        if not first:
            old_direction, old_rho = refs[:2]
            refs = refs[2:]
        inner = None
        if not last:
            inner = refs[0]
            refs = refs[1:]
        payload, direction, rho, sep, split, sem = refs
        copy = pltpu.make_async_copy(sep_vmem, sep, sem)
        copy.start()
        acc = middle[...] + coarse_back((3, 4), (sum3, sum4), PRE, coupling, place)
        rho_new = side_totals(square)
        if not first:
            ratio = rho_new / old_rho[...]
        rho[...] = rho_new
        vec = []
        for k in range(NB):
            tile = acc[8 * k : 8 * k + 8]
            if not first:
                tile = tile + ratio * tile_of(old_direction, k)
            tile = keep_sides(tile)
            direction[8 * k : 8 * k + 8, :] = tile
            split[k] = split_rows(tile)
            vec.append(tile)
        copy.wait()
        contributions(flipped, sep, split, payload)
        payload[LEVELS * ROWS :, :] = local_square(vec, own_diag(shunt), 1.0, factor, inner)

    return kernel


def make_operator_kernel(first):
    def kernel(sep_vmem, sum3, sum4, square, middle, shunt, factor, coupling, flipped, place, *refs):
        direction, residual, rho = refs[:3]
        refs = refs[3:]
        if not first:
            estimate = refs[0]
            refs = refs[1:]
        inner, payload, next_residual, next_estimate, sep, split, sem = refs
        copy = pltpu.make_async_copy(sep_vmem, sep, sem)
        copy.start()
        acc = middle[...] + coarse_back((3, 4), (sum3, sum4), OP, coupling, place)
        step = rho[...] / side_totals(square)
        vec = []
        for k in range(NB):
            tile = keep_sides(tile_of(residual, k) - step * acc[8 * k : 8 * k + 8])
            next_residual[8 * k : 8 * k + 8, :] = tile
            split[k] = split_rows(tile)
            vec.append(tile)
        copy.wait()
        contributions(flipped, sep, split, payload)
        payload[LEVELS * ROWS :, :] = local_square(vec, pre_diag(shunt), 0.25, factor, inner)
        for k in range(NB):
            gain = step * tile_of(direction, k)
            next_estimate[8 * k : 8 * k + 8, :] = gain if first else tile_of(estimate, k) + gain

    return kernel


def drops_kernel(vec, ends, drops):
    def chunk(i, carry):
        here = pl.ds(pl.multiple_of(8 * i, 8), 8)

        def at(end):
            index = ends[end, here, :]
            block = index >> 7
            lane = index & (W - 1)
            values = [jnp.zeros((8, W), F32)] * 2
            for k in range(NB):
                chosen = block == k
                for side in range(2):
                    row = jnp.broadcast_to(vec[8 * k + side : 8 * k + side + 1, :], (8, W))
                    found = jnp.take_along_axis(row, lane, axis=1)
                    values[side] = jnp.where(chosen, found, values[side])
            return values

        low, high = at(0), at(1)
        for side in range(2):
            drops[side, here, :] = low[side] - high[side]
        return carry

    lax.fori_loop(0, drops.shape[1] // 8, chunk, 0)


def last_kernel(square, direction, rho, estimate, known, change, volts, terms):
    step = rho[...] / side_totals(square)
    for side in range(2):
        gain = jnp.broadcast_to(step[side : side + 1, :], (8, W))
        if side == 0:
            forward = gain
        else:
            adjoint = gain
    for i in range(terms.shape[0] // 8):
        here = slice(8 * i, 8 * i + 8)
        drop = known[0, here, :] + forward * change[0, here, :]
        back = known[1, here, :] + adjoint * change[1, here, :]
        terms[here, :] = -(back * drop)
    for k in range(NB):
        tile = tile_of(estimate, k) + step * tile_of(direction, k)
        volts[0, k : k + 1, :] = tile[0:1]
        volts[1, k : k + 1, :] = tile[1:2]


TILES = jax.ShapeDtypeStruct((FLAT, W), F32)
PAYLOAD = jax.ShapeDtypeStruct((LEVELS * ROWS + 8, W), F32)
TILE = jax.ShapeDtypeStruct((8, W), F32)
INNER = jax.ShapeDtypeStruct((NB, 16, W), BF16)
COUPLING = jax.ShapeDtypeStruct((LEVELS * NB, 2 * W, W), BF16)
FACTOR = jax.ShapeDtypeStruct((NB, 2 * W, W), BF16)
PLACE = jax.ShapeDtypeStruct((FLAT, 256), BF16)
PLACE_TWO = jax.ShapeDtypeStruct((FLAT, 4 * FLAT), BF16)
SEP_SCRATCH = [
    pltpu.SMEM((LEVELS, NB), jnp.int32),
    pltpu.VMEM((NB, 16, W), BF16),
    pltpu.SemaphoreType.DMA,
]


def call(kernel, name, args, outs, scratch=(), smem=0, hbm=(), limit=16):
    specs = [SMEM if i < smem else HBM if i in hbm else VMEM for i in range(len(args))]
    one = not isinstance(outs, list)
    return pl.pallas_call(
        kernel,
        in_specs=specs,
        out_specs=VMEM if one else [VMEM] * len(outs),
        out_shape=outs,
        scratch_shapes=list(scratch),
        compiler_params=pltpu.CompilerParams(vmem_limit_bytes=limit * MIB),
        name=name,
    )(*args)


OTHER_QUAD = {0: 6, 1: 7, 2: 4, 3: 5, 4: 2, 5: 3, 6: 0, 7: 1}


def partners(kind, count):
    if kind == "other":
        return [(s, s // 8 * 8 + OTHER_QUAD[s % 8]) for s in range(count)]
    return [(s, s ^ kind) for s in range(count)]


def power(rows):
    return rows[:8] * rows[:8] + rows[8:16] * rows[8:16] + rows[16:] * rows[16:]


def tree_exchange(payload, weights, jobs):
    count = lax.axis_size("dom")

    def fetch(value, kinds, number, finished, results):
        got = [lax.ppermute(value, "dom", partners(kind, count)) for kind in kinds]
        if number in jobs:
            results[number] = jobs[number](finished, results)
            got, results[number] = lax.optimization_barrier((got, results[number]))
            return got
        return lax.optimization_barrier(got)

    def quad(value, kinds, number, finished, results, level):
        farther, far, near = fetch(value, kinds, number, finished, results)
        pair = value[:-8] + near[:-8]
        other = far[:-8] + farther[:-8]
        low = pair[:ROWS]
        both = pair[ROWS:] + other[ROWS:]
        high = both[:ROWS]
        square = (value[-8:] + near[-8:]) + (far[-8:] + farther[-8:])
        square = square + weights[level] * (power(low) + power(other[:ROWS]))
        square = square + weights[level + 1] * power(high)
        return low, high, both[ROWS:], square

    results = {}
    low, high, pending, square = quad(payload, (3, 2, 1), 0, [], results, 0)
    finished = [low, high]
    pending = jnp.concatenate([pending, square], axis=0)
    (received,) = fetch(pending, ("other",), 1, finished, results)
    total = pending + received
    finished.append(total[:ROWS])
    square = total[-8:] + weights[2] * power(total[:ROWS])
    pending = jnp.concatenate([total[ROWS:-8], square], axis=0)
    low, high, _, square = quad(pending, (16, 24, 8), 2, finished, results, 3)
    return low, high, square, results


def shards(
    load_current, worst_node, cond_diag, branch, precond_factor, coupling, sep_map, strap_ends
):
    node_count = NB * W
    shunt = cond_diag.reshape(NB, W)
    target = worst_node - lax.axis_index("dom") * node_count
    target = jnp.broadcast_to(target[:, None], (1, W))
    ends = strap_ends.reshape(2, -1, W)
    strap_rows = ends.shape[1]
    drops_shape = jax.ShapeDtypeStruct(ends.shape, F32)

    payload, inner, residual, cpl, pre, place01, place2, place34 = call(
        first_kernel,
        "first_part",
        (
            pltpu.with_memory_space_constraint(sep_map, pltpu.HBM),
            target,
            pltpu.with_memory_space_constraint(load_current, pltpu.HBM),
            pltpu.with_memory_space_constraint(shunt, pltpu.HBM),
            pltpu.with_memory_space_constraint(coupling.reshape(LEVELS * NB, W, W), pltpu.HBM),
            pltpu.with_memory_space_constraint(precond_factor, pltpu.HBM),
        ),
        [PAYLOAD, INNER, TILES, COUPLING, FACTOR, PLACE_TWO, PLACE, PLACE_TWO],
        [
            pltpu.SMEM((LEVELS, NB), jnp.int32),
            pltpu.VMEM((1, node_count), F32),
            pltpu.VMEM((NB, W), F32),
            pltpu.VMEM((LEVELS * NB, W, W), F32),
            pltpu.VMEM((NB, W, W), F32),
            pltpu.VMEM((NB, 16, W), BF16),
            pltpu.SemaphoreType.DMA((4,)),
            pltpu.SemaphoreType.DMA((LEVELS * NB // CHUNK,)),
        ],
        hbm=(0, 2, 3, 4, 5),
        limit=24,
    )
    direction = rho = estimate = flipped = brn = None

    def exchange(payload, precond, vec, inner, factor, jobs, back=True):
        def early(finished, results):
            args = (finished[0], finished[1], vec, inner, shunt, factor, cpl, place01)
            return call(make_early_kernel(precond), "early_levels", args, TILES)

        def middle(finished, results):
            args = (finished[2], results[1], cpl, place2)
            return call(make_middle_kernel(precond), "middle_level", args, TILES)

        if back:
            jobs = {**jobs, 1: early, 2: middle}
        return tree_exchange(payload, PRE if precond else OP, jobs)

    for iteration in range(ITERS):
        first = iteration == 0
        last = iteration + 1 == ITERS
        jobs = {}
        if first:
            jobs[0] = lambda *_: (
                call(split_kernel, "split_branch", (branch,), FACTOR),
                call(transpose_kernel, "flip", (cpl,), COUPLING),
            )
        if last:
            jobs[0] = lambda *_: call(drops_kernel, "known", (estimate, ends), drops_shape)
        sum3, sum4, square, results = exchange(payload, True, residual, inner, pre, jobs)
        if first:
            brn, flipped = results[0]
        if last:
            known = results[0]
        args = (sep_map, sum3, sum4, square, results[2], shunt, brn, cpl, flipped, place34)
        if not first:
            args += (direction, rho)
        outs = [PAYLOAD, TILES, TILE]
        *inner, payload, direction, rho = call(
            make_precond_kernel(first, last),
            "precond_round",
            args,
            outs if last else [INNER] + outs,
            SEP_SCRATCH,
        )
        inner = None if last else inner[0]
        jobs = {}
        if last:
            jobs[0] = lambda *_: call(drops_kernel, "change", (direction, ends), drops_shape)
        sum3, sum4, square, results = exchange(
            payload, False, direction, inner, brn, jobs, not last
        )
        if last:
            change = results[0]
        else:
            args = (sep_map, sum3, sum4, square, results[2], shunt, pre, cpl, flipped, place34)
            args += (direction, residual, rho)
            if not first:
                args += (estimate,)
            inner, payload, residual, estimate = call(
                make_operator_kernel(first),
                "operator_round",
                args,
                [INNER, PAYLOAD, TILES, TILES],
                SEP_SCRATCH,
            )
    volts, terms = call(
        last_kernel,
        "straps",
        (square, direction, rho, estimate, known, change),
        [
            jax.ShapeDtypeStruct((2, NB, W), F32),
            jax.ShapeDtypeStruct((strap_rows, W), F32),
        ],
    )
    terms = terms + lax.ppermute(terms, "load", [(s, s ^ 1) for s in range(8)])
    near, far, farther = [
        lax.ppermute(terms, "load", [(s, s ^ mask) for s in range(8)]) for mask in (2, 4, 6)
    ]
    terms = (terms + near) + (far + farther)
    return (volts.reshape(2, 1, node_count), terms.reshape(-1))


def solution(mesh):
    placed = (
        P("load", "dom"),
        P("load"),
        P("dom"),
        P("dom", None, None),
        P("dom", None, None),
        P(None, "dom", None, None),
        P(None, "dom"),
        P(None, "dom"),
    )
    return jax.shard_map(
        shards,
        mesh=mesh,
        in_specs=placed,
        out_specs=(P(None, "load", "dom"), P("dom")),
        check_vma=False,
    )
```

```python
import math

import jax
import jax.numpy as jnp
from jax import lax
from jax.experimental import pallas as pl
from jax.experimental.pallas import tpu as pltpu
from jax.sharding import PartitionSpec as P

ITERS = 4
LEVELS = 5
NB = 12
W = 128
ROWS = 2 * NB
FLAT = 8 * NB
CHUNK = 20
OP = [1.0 / math.sqrt(2.0 ** (level + 1)) for level in range(LEVELS)]
PRE = [0.5 * c for c in OP]
F32 = jnp.float32
BF16 = jnp.bfloat16
VMEM = pl.BlockSpec(memory_space=pltpu.VMEM)
HBM = pl.BlockSpec(memory_space=pltpu.HBM)
MIB = 1024 * 1024


def split_rows(tile):
    high = tile.astype(BF16).astype(F32)
    return jnp.concatenate([high, tile - high], axis=0).astype(BF16)


def times(rows, matrix):
    out = lax.dot_general(
        jnp.concatenate([rows, rows], axis=1),
        matrix,
        (((1,), (0,)), ((), ())),
        preferred_element_type=F32,
    )
    return out[:8] + out[8:]


def times_t(rows, matrix):
    out = lax.dot_general(rows, matrix, (((1,), (1,)), ((), ())), preferred_element_type=F32)
    out = out[:8] + out[8:]
    return out[:, :W] + out[:, W:]


def store_split(mats, out, index):
    high = mats.astype(BF16)
    out[index, :W, :] = high
    out[index, W:, :] = (mats - high.astype(F32)).astype(BF16)


def split_kernel(mat_ref, out_ref):
    for j in range(NB):
        store_split(mat_ref[j], out_ref, j)


def transpose_kernel(coupling, flipped):
    row = lax.broadcasted_iota(jnp.int32, (W, W), 0)
    eye = (row == lax.broadcasted_iota(jnp.int32, (W, W), 1)).astype(F32).astype(BF16)
    for i in range(LEVELS * NB):
        out = lax.dot_general(
            eye, coupling[i], (((1,), (1,)), ((), ())), preferred_element_type=F32
        ).astype(BF16)
        flipped[i, :W, :] = out[:, :W]
        flipped[i, W:, :] = out[:, W:]


def side_totals(square):
    total = square[...]
    total = total + pltpu.roll(total, 2, 0)
    total = total + pltpu.roll(total, 4, 0)
    return jnp.broadcast_to(jnp.sum(total, axis=1, keepdims=True), (8, W))


def keep_sides(tile):
    return jnp.where(lax.broadcasted_iota(jnp.int32, (8, W), 0) < 2, tile, 0.0)


def tile_of(ref, k):
    return ref[8 * k : 8 * k + 8, :]


def stacked(values):
    high = values.astype(BF16).astype(F32)
    parts = [high, values - high]
    spare = -2 * values.shape[0] % W
    if spare:
        parts.append(jnp.zeros((spare, W), F32))
    return jnp.concatenate(parts, axis=0).astype(BF16)


def dot(left, right):
    return lax.dot_general(left, right, (((1,), (0,)), ((), ())), preferred_element_type=F32)


def place_matrix(sep, levels):
    used = FLAT * len(levels)
    width = 2 * used + -2 * used % W
    row = lax.broadcasted_iota(jnp.int32, (8, width), 0)
    col = lax.broadcasted_iota(jnp.int32, (8, width), 1)
    inside = jnp.where(col >= used, col - used, col)
    number = jnp.where(inside >= FLAT, 1, 0)
    inside = inside - FLAT * number
    block = inside >> 3
    valid = (row < 2) & (col < 2 * used) & ((inside & 7) == 2 * (block & 3) + row)
    owner = jnp.full((8, width), -1, jnp.int32)
    for n, level in enumerate(levels):
        for j in range(NB):
            owner = jnp.where(valid & (number == n) & (block == j), sep[level, j], owner)
    tiles = [jnp.where(owner == k, 1.0, 0.0) for k in range(NB)]
    return jnp.concatenate(tiles, axis=0).astype(BF16)


def coarse_back(levels, totals, weights, coupling, place):
    outs = []
    for level, total in zip(levels, totals):
        for group in range(NB // 4):
            rows = split_rows(total[8 * group : 8 * group + 8, :] * weights[level])
            for member in range(4):
                outs.append(times(rows, coupling[level * NB + 4 * group + member]))
    return dot(place[...], stacked(jnp.concatenate(outs, axis=0)))


def local_square(vec, diag, scale, factor, inner_out):
    square = jnp.zeros((8, W), F32)
    for k in range(NB):
        inner = times(split_rows(vec[k]), factor[k])
        if inner_out is not None:
            inner_out[k] = split_rows(inner)
        square = square + (diag[k] * vec[k] * vec[k] + scale * (inner * inner))
    return square


def put(payload, level, j, out):
    payload[level * ROWS + 2 * j : level * ROWS + 2 * j + 2, :] = out[0:2]


def contributions(flipped, sep, split, payload):
    for level in range(LEVELS):
        for j in range(NB):
            put(payload, level, j, times(split[sep[level, j]], flipped[level * NB + j]))


def own_diag(shunt):
    return [jnp.broadcast_to(shunt[k : k + 1, :], (8, W)) for k in range(NB)]


def pre_diag(shunt):
    return [1.0 / (tile + 1.0) for tile in own_diag(shunt)]


def first_kernel(
    sep_hbm,
    target,
    load_hbm,
    shunt_hbm,
    coupling_hbm,
    factor_hbm,
    payload,
    inner_out,
    vec_out,
    coupling,
    factor,
    place01,
    place2,
    place34,
    sep,
    load,
    shunt,
    raw,
    raw_factor,
    split,
    small_sems,
    sems,
):
    small = [
        pltpu.make_async_copy(source, place, small_sems.at[n])
        for n, (source, place) in enumerate(
            ((sep_hbm, sep), (load_hbm, load), (shunt_hbm, shunt), (factor_hbm, raw_factor))
        )
    ]
    copies = [
        pltpu.make_async_copy(
            coupling_hbm.at[pl.ds(n * CHUNK, CHUNK)], raw.at[pl.ds(n * CHUNK, CHUNK)], sems.at[n]
        )
        for n in range(LEVELS * NB // CHUNK)
    ]
    for copy in small[:3] + copies + small[3:]:
        copy.start()
    small[1].wait()
    side = lax.broadcasted_iota(jnp.int32, (8, W), 0)
    lane = lax.broadcasted_iota(jnp.int32, (8, W), 1)
    goal = jnp.broadcast_to(target[...], (8, W))
    vec = []
    for k in range(NB):
        unit = jnp.where((side == 1) & (lane + k * W == goal), 1.0, 0.0)
        row = jnp.broadcast_to(load[0:1, k * W : (k + 1) * W], (8, W))
        tile = jnp.where(side == 0, row, unit)
        vec_out[8 * k : 8 * k + 8, :] = tile
        split[k] = split_rows(tile)
        vec.append(tile)
    small[0].wait()
    place01[...] = place_matrix(sep, (0, 1))
    place2[...] = place_matrix(sep, (2,))
    place34[...] = place_matrix(sep, (3, 4))
    for n, copy in enumerate(copies):
        copy.wait()
        for i in range(n * CHUNK, (n + 1) * CHUNK):
            store_split(raw[i], coupling, i)
        for i in range(n * CHUNK, (n + 1) * CHUNK):
            level, j = divmod(i, NB)
            put(payload, level, j, times_t(split[sep[level, j]], coupling[i]))
    small[2].wait()
    small[3].wait()
    for k in range(NB):
        store_split(raw_factor[k], factor, k)
    payload[LEVELS * ROWS :, :] = local_square(vec, pre_diag(shunt), 0.25, factor, inner_out)


def make_early_kernel(precond):
    def kernel(sum0, sum1, vec, inner, shunt, factor, coupling, place, acc):
        weights = PRE if precond else OP
        diag = pre_diag(shunt) if precond else own_diag(shunt)
        scale = 0.25 if precond else 1.0
        tiles = [
            diag[k] * tile_of(vec, k) + scale * times_t(inner[k], factor[k]) for k in range(NB)
        ]
        back = coarse_back((0, 1), (sum0, sum1), weights, coupling, place)
        acc[...] = back + jnp.concatenate(tiles, axis=0)

    return kernel


def make_middle_kernel(precond):
    def kernel(sum2, early, coupling, place, acc):
        weights = PRE if precond else OP
        acc[...] = early[...] + coarse_back((2,), (sum2,), weights, coupling, place)

    return kernel


def make_precond_kernel(first, last):
    def kernel(sep_vmem, sum3, sum4, square, middle, shunt, factor, coupling, flipped, place, *refs):
        if not first:
            old_direction, old_rho = refs[:2]
            refs = refs[2:]
        inner = None
        if not last:
            inner = refs[0]
            refs = refs[1:]
        payload, direction, rho, sep, split, sem = refs
        copy = pltpu.make_async_copy(sep_vmem, sep, sem)
        copy.start()
        acc = middle[...] + coarse_back((3, 4), (sum3, sum4), PRE, coupling, place)
        rho_new = side_totals(square)
        if not first:
            ratio = rho_new / old_rho[...]
        rho[...] = rho_new
        vec = []
        for k in range(NB):
            tile = acc[8 * k : 8 * k + 8]
            if not first:
                tile = tile + ratio * tile_of(old_direction, k)
            tile = keep_sides(tile)
            direction[8 * k : 8 * k + 8, :] = tile
            split[k] = split_rows(tile)
            vec.append(tile)
        copy.wait()
        contributions(flipped, sep, split, payload)
        payload[LEVELS * ROWS :, :] = local_square(vec, own_diag(shunt), 1.0, factor, inner)

    return kernel


def operator_kernel(
    sep_vmem,
    sum3,
    sum4,
    square,
    middle,
    shunt,
    factor,
    coupling,
    flipped,
    place,
    residual,
    rho,
    inner,
    payload,
    next_residual,
    step_out,
    sep,
    split,
    sem,
):
    copy = pltpu.make_async_copy(sep_vmem, sep, sem)
    copy.start()
    acc = middle[...] + coarse_back((3, 4), (sum3, sum4), OP, coupling, place)
    step = rho[...] / side_totals(square)
    step_out[...] = step
    vec = []
    for k in range(NB):
        tile = keep_sides(tile_of(residual, k) - step * acc[8 * k : 8 * k + 8])
        next_residual[8 * k : 8 * k + 8, :] = tile
        split[k] = split_rows(tile)
        vec.append(tile)
    copy.wait()
    contributions(flipped, sep, split, payload)
    payload[LEVELS * ROWS :, :] = local_square(vec, pre_diag(shunt), 0.25, factor, inner)


def make_update_kernel(first):
    def kernel(step, direction, *refs):
        for k in range(NB):
            tile = step[...] * tile_of(direction, k)
            if not first:
                tile = tile + tile_of(refs[0], k)
            refs[-1][8 * k : 8 * k + 8, :] = tile

    return kernel


def drops_kernel(vec, ends, drops):
    def chunk(i, carry):
        here = pl.ds(pl.multiple_of(8 * i, 8), 8)

        def at(end):
            index = ends[end, here, :]
            block = index >> 7
            lane = index & (W - 1)
            values = [jnp.zeros((8, W), F32)] * 2
            for k in range(NB):
                chosen = block == k
                for side in range(2):
                    row = jnp.broadcast_to(vec[8 * k + side : 8 * k + side + 1, :], (8, W))
                    found = jnp.take_along_axis(row, lane, axis=1)
                    values[side] = jnp.where(chosen, found, values[side])
            return values

        low, high = at(0), at(1)
        for side in range(2):
            drops[side, here, :] = low[side] - high[side]
        return carry

    lax.fori_loop(0, drops.shape[1] // 8, chunk, 0)


def last_kernel(square, direction, rho, estimate, known, change, volts, terms):
    step = rho[...] / side_totals(square)
    for side in range(2):
        gain = jnp.broadcast_to(step[side : side + 1, :], (8, W))
        if side == 0:
            forward = gain
        else:
            adjoint = gain
    for i in range(terms.shape[0] // 8):
        here = slice(8 * i, 8 * i + 8)
        drop = known[0, here, :] + forward * change[0, here, :]
        back = known[1, here, :] + adjoint * change[1, here, :]
        terms[here, :] = -(back * drop)
    for k in range(NB):
        tile = tile_of(estimate, k) + step * tile_of(direction, k)
        volts[0, k : k + 1, :] = tile[0:1]
        volts[1, k : k + 1, :] = tile[1:2]


TILES = jax.ShapeDtypeStruct((FLAT, W), F32)
PAYLOAD = jax.ShapeDtypeStruct((LEVELS * ROWS + 8, W), F32)
TILE = jax.ShapeDtypeStruct((8, W), F32)
INNER = jax.ShapeDtypeStruct((NB, 16, W), BF16)
COUPLING = jax.ShapeDtypeStruct((LEVELS * NB, 2 * W, W), BF16)
FACTOR = jax.ShapeDtypeStruct((NB, 2 * W, W), BF16)
PLACE = jax.ShapeDtypeStruct((FLAT, 256), BF16)
PLACE_TWO = jax.ShapeDtypeStruct((FLAT, 4 * FLAT), BF16)
SEP_SCRATCH = [
    pltpu.SMEM((LEVELS, NB), jnp.int32),
    pltpu.VMEM((NB, 16, W), BF16),
    pltpu.SemaphoreType.DMA,
]


def call(kernel, name, args, outs, scratch=(), hbm=(), limit=16):
    specs = [HBM if i in hbm else VMEM for i in range(len(args))]
    one = not isinstance(outs, list)
    return pl.pallas_call(
        kernel,
        in_specs=specs,
        out_specs=VMEM if one else [VMEM] * len(outs),
        out_shape=outs,
        scratch_shapes=list(scratch),
        compiler_params=pltpu.CompilerParams(vmem_limit_bytes=limit * MIB),
        name=name,
    )(*args)


OTHER_QUAD = {0: 6, 1: 7, 2: 4, 3: 5, 4: 2, 5: 3, 6: 0, 7: 1}


def partners(kind, count):
    if kind == "other":
        return [(s, s // 8 * 8 + OTHER_QUAD[s % 8]) for s in range(count)]
    return [(s, s ^ kind) for s in range(count)]


def power(rows):
    return rows[:8] * rows[:8] + rows[8:16] * rows[8:16] + rows[16:] * rows[16:]


def tree_exchange(payload, weights, jobs):
    count = lax.axis_size("dom")

    def fetch(value, kinds, number, finished, results):
        got = [lax.ppermute(value, "dom", partners(kind, count)) for kind in kinds]
        if number in jobs:
            results[number] = jobs[number](finished, results)
            got, results[number] = lax.optimization_barrier((got, results[number]))
            return got
        return lax.optimization_barrier(got)

    def quad(value, kinds, number, finished, results, level):
        farther, far, near = fetch(value, kinds, number, finished, results)
        pair = value[:-8] + near[:-8]
        other = far[:-8] + farther[:-8]
        low = pair[:ROWS]
        both = pair[ROWS:] + other[ROWS:]
        high = both[:ROWS]
        square = (value[-8:] + near[-8:]) + (far[-8:] + farther[-8:])
        square = square + weights[level] * (power(low) + power(other[:ROWS]))
        square = square + weights[level + 1] * power(high)
        return low, high, both[ROWS:], square

    results = {}
    low, high, pending, square = quad(payload, (3, 2, 1), 0, [], results, 0)
    finished = [low, high]
    pending = jnp.concatenate([pending, square], axis=0)
    (received,) = fetch(pending, ("other",), 1, finished, results)
    total = pending + received
    finished.append(total[:ROWS])
    square = total[-8:] + weights[2] * power(total[:ROWS])
    pending = jnp.concatenate([total[ROWS:-8], square], axis=0)
    low, high, _, square = quad(pending, (16, 24, 8), 2, finished, results, 3)
    return low, high, square, results


def shards(
    load_current, worst_node, cond_diag, branch, precond_factor, coupling, sep_map, strap_ends
):
    node_count = NB * W
    shunt = cond_diag.reshape(NB, W)
    target = worst_node - lax.axis_index("dom") * node_count
    target = jnp.broadcast_to(target[:, None], (1, W))
    ends = strap_ends.reshape(2, -1, W)
    strap_rows = ends.shape[1]
    drops_shape = jax.ShapeDtypeStruct(ends.shape, F32)

    payload, inner, residual, cpl, pre, place01, place2, place34 = call(
        first_kernel,
        "first_part",
        (
            pltpu.with_memory_space_constraint(sep_map, pltpu.HBM),
            target,
            pltpu.with_memory_space_constraint(load_current, pltpu.HBM),
            pltpu.with_memory_space_constraint(shunt, pltpu.HBM),
            pltpu.with_memory_space_constraint(coupling.reshape(LEVELS * NB, W, W), pltpu.HBM),
            pltpu.with_memory_space_constraint(precond_factor, pltpu.HBM),
        ),
        [PAYLOAD, INNER, TILES, COUPLING, FACTOR, PLACE_TWO, PLACE, PLACE_TWO],
        [
            pltpu.SMEM((LEVELS, NB), jnp.int32),
            pltpu.VMEM((1, node_count), F32),
            pltpu.VMEM((NB, W), F32),
            pltpu.VMEM((LEVELS * NB, W, W), F32),
            pltpu.VMEM((NB, W, W), F32),
            pltpu.VMEM((NB, 16, W), BF16),
            pltpu.SemaphoreType.DMA((4,)),
            pltpu.SemaphoreType.DMA((LEVELS * NB // CHUNK,)),
        ],
        hbm=(0, 2, 3, 4, 5),
        limit=24,
    )
    direction = rho = estimate = flipped = brn = step = None

    def exchange(payload, precond, vec, inner, factor, jobs, back=True):
        def early(finished, results):
            args = (finished[0], finished[1], vec, inner, shunt, factor, cpl, place01)
            return call(make_early_kernel(precond), "early_levels", args, TILES)

        def middle(finished, results):
            args = (finished[2], results[1], cpl, place2)
            return call(make_middle_kernel(precond), "middle_level", args, TILES)

        if back:
            jobs = {**jobs, 1: early, 2: middle}
        return tree_exchange(payload, PRE if precond else OP, jobs)

    for iteration in range(ITERS):
        first = iteration == 0
        last = iteration + 1 == ITERS
        jobs = {}
        if first:
            jobs[0] = lambda *_: (
                call(split_kernel, "split_branch", (branch,), FACTOR),
                call(transpose_kernel, "flip", (cpl,), COUPLING),
            )
        else:

            def update(*_):
                begun = () if estimate is None else (estimate,)
                args = (step, direction) + begun
                new = call(make_update_kernel(not begun), "update", args, TILES)
                if last:
                    return new, call(drops_kernel, "known", (new, ends), drops_shape)
                return (new,)

            jobs[0] = update
        sum3, sum4, square, results = exchange(payload, True, residual, inner, pre, jobs)
        if first:
            brn, flipped = results[0]
        else:
            estimate = results[0][0]
        if last:
            known = results[0][1]
        args = (sep_map, sum3, sum4, square, results[2], shunt, brn, cpl, flipped, place34)
        if not first:
            args += (direction, rho)
        outs = [PAYLOAD, TILES, TILE]
        *inner, payload, direction, rho = call(
            make_precond_kernel(first, last),
            "precond_round",
            args,
            outs if last else [INNER] + outs,
            SEP_SCRATCH,
        )
        inner = None if last else inner[0]
        jobs = {}
        if last:
            jobs[0] = lambda *_: call(drops_kernel, "change", (direction, ends), drops_shape)
        sum3, sum4, square, results = exchange(
            payload, False, direction, inner, brn, jobs, not last
        )
        if last:
            change = results[0]
        else:
            args = (sep_map, sum3, sum4, square, results[2], shunt, pre, cpl, flipped, place34)
            inner, payload, residual, step = call(
                operator_kernel,
                "operator_round",
                (*args, residual, rho),
                [INNER, PAYLOAD, TILES, TILE],
                SEP_SCRATCH,
            )
    volts, terms = call(
        last_kernel,
        "straps",
        (square, direction, rho, estimate, known, change),
        [
            jax.ShapeDtypeStruct((2, NB, W), F32),
            jax.ShapeDtypeStruct((strap_rows, W), F32),
        ],
    )
    terms = terms + lax.ppermute(terms, "load", [(s, s ^ 1) for s in range(8)])
    near, far, farther = [
        lax.ppermute(terms, "load", [(s, s ^ mask) for s in range(8)]) for mask in (2, 4, 6)
    ]
    terms = (terms + near) + (far + farther)
    return (volts.reshape(2, 1, node_count), terms.reshape(-1))


def solution(mesh):
    placed = (
        P("load", "dom"),
        P("load"),
        P("dom"),
        P("dom", None, None),
        P("dom", None, None),
        P(None, "dom", None, None),
        P(None, "dom"),
        P(None, "dom"),
    )
    return jax.shard_map(
        shards,
        mesh=mesh,
        in_specs=placed,
        out_specs=(P(None, "load", "dom"), P("dom")),
        check_vma=False,
    )
```

```python
import math

import jax
import jax.numpy as jnp
from jax import lax
from jax.experimental import pallas as pl
from jax.experimental.pallas import tpu as pltpu
from jax.sharding import PartitionSpec as P

ITERS = 4
LEVELS = 5
NB = 12
W = 128
ROWS = 2 * NB
FLAT = 8 * NB
CHUNK = 20
OP = [1.0 / math.sqrt(2.0 ** (level + 1)) for level in range(LEVELS)]
PRE = [0.5 * c for c in OP]
F32 = jnp.float32
BF16 = jnp.bfloat16
VMEM = pl.BlockSpec(memory_space=pltpu.VMEM)
HBM = pl.BlockSpec(memory_space=pltpu.HBM)
MIB = 1024 * 1024


def split_rows(tile):
    high = tile.astype(BF16).astype(F32)
    return jnp.concatenate([high, tile - high], axis=0).astype(BF16)


def times(rows, matrix):
    out = lax.dot_general(
        jnp.concatenate([rows, rows], axis=1),
        matrix,
        (((1,), (0,)), ((), ())),
        preferred_element_type=F32,
    )
    return out[:8] + out[8:]


def times_t(rows, matrix):
    out = lax.dot_general(rows, matrix, (((1,), (1,)), ((), ())), preferred_element_type=F32)
    out = out[:8] + out[8:]
    return out[:, :W] + out[:, W:]


def store_split(mats, out, index):
    high = mats.astype(BF16)
    out[index, :W, :] = high
    out[index, W:, :] = (mats - high.astype(F32)).astype(BF16)


def split_kernel(mat_ref, out_ref):
    for j in range(NB):
        store_split(mat_ref[j], out_ref, j)


def transpose_kernel(coupling, flipped):
    row = lax.broadcasted_iota(jnp.int32, (W, W), 0)
    eye = (row == lax.broadcasted_iota(jnp.int32, (W, W), 1)).astype(F32).astype(BF16)
    for i in range(LEVELS * NB):
        out = lax.dot_general(
            eye, coupling[i], (((1,), (1,)), ((), ())), preferred_element_type=F32
        ).astype(BF16)
        flipped[i, :W, :] = out[:, :W]
        flipped[i, W:, :] = out[:, W:]


def side_totals(square):
    total = square[...]
    total = total + pltpu.roll(total, 2, 0)
    total = total + pltpu.roll(total, 4, 0)
    return jnp.broadcast_to(jnp.sum(total, axis=1, keepdims=True), (8, W))


def keep_sides(tile):
    return jnp.where(lax.broadcasted_iota(jnp.int32, (8, W), 0) < 2, tile, 0.0)


def tile_of(ref, k):
    return ref[8 * k : 8 * k + 8, :]


def stacked(values):
    high = values.astype(BF16).astype(F32)
    parts = [high, values - high]
    spare = -2 * values.shape[0] % W
    if spare:
        parts.append(jnp.zeros((spare, W), F32))
    return jnp.concatenate(parts, axis=0).astype(BF16)


def dot(left, right):
    return lax.dot_general(left, right, (((1,), (0,)), ((), ())), preferred_element_type=F32)


def place_matrix(sep, levels):
    used = FLAT * len(levels)
    width = 2 * used + -2 * used % W
    row = lax.broadcasted_iota(jnp.int32, (8, width), 0)
    col = lax.broadcasted_iota(jnp.int32, (8, width), 1)
    inside = jnp.where(col >= used, col - used, col)
    number = jnp.where(inside >= FLAT, 1, 0)
    inside = inside - FLAT * number
    block = inside >> 3
    valid = (row < 2) & (col < 2 * used) & ((inside & 7) == 2 * (block & 3) + row)
    owner = jnp.full((8, width), -1, jnp.int32)
    for n, level in enumerate(levels):
        for j in range(NB):
            owner = jnp.where(valid & (number == n) & (block == j), sep[level, j], owner)
    tiles = [jnp.where(owner == k, 1.0, 0.0) for k in range(NB)]
    return jnp.concatenate(tiles, axis=0).astype(BF16)


def coarse_back(levels, totals, weights, coupling, place):
    outs = []
    for level, total in zip(levels, totals):
        for group in range(NB // 4):
            rows = split_rows(total[8 * group : 8 * group + 8, :] * weights[level])
            for member in range(4):
                outs.append(times(rows, coupling[level * NB + 4 * group + member]))
    return dot(place[...], stacked(jnp.concatenate(outs, axis=0)))


def local_square(vec, diag, scale, factor, inner_out):
    square = jnp.zeros((8, W), F32)
    for k in range(NB):
        inner = times(split_rows(vec[k]), factor[k])
        if inner_out is not None:
            inner_out[k] = split_rows(inner)
        square = square + (diag[k] * vec[k] * vec[k] + scale * (inner * inner))
    return square


def put(payload, level, j, out):
    payload[level * ROWS + 2 * j : level * ROWS + 2 * j + 2, :] = out[0:2]


def contributions(flipped, sep, split, payload):
    for level in range(LEVELS):
        for j in range(NB):
            put(payload, level, j, times(split[sep[level, j]], flipped[level * NB + j]))


def own_diag(shunt):
    return [jnp.broadcast_to(shunt[k : k + 1, :], (8, W)) for k in range(NB)]


def pre_diag(shunt):
    return [1.0 / (tile + 1.0) for tile in own_diag(shunt)]


def first_kernel(
    sep_hbm,
    target,
    load_hbm,
    shunt_hbm,
    coupling_hbm,
    factor_hbm,
    payload,
    inner_out,
    vec_out,
    coupling,
    factor,
    place01,
    place2,
    place34,
    sep,
    load,
    shunt,
    raw,
    raw_factor,
    split,
    small_sems,
    sems,
):
    small = [
        pltpu.make_async_copy(source, place, small_sems.at[n])
        for n, (source, place) in enumerate(
            ((sep_hbm, sep), (load_hbm, load), (shunt_hbm, shunt), (factor_hbm, raw_factor))
        )
    ]
    copies = [
        pltpu.make_async_copy(
            coupling_hbm.at[pl.ds(n * CHUNK, CHUNK)], raw.at[pl.ds(n * CHUNK, CHUNK)], sems.at[n]
        )
        for n in range(LEVELS * NB // CHUNK)
    ]
    for copy in small[:3] + copies + small[3:]:
        copy.start()
    small[1].wait()
    side = lax.broadcasted_iota(jnp.int32, (8, W), 0)
    lane = lax.broadcasted_iota(jnp.int32, (8, W), 1)
    goal = jnp.broadcast_to(target[...], (8, W))
    vec = []
    for k in range(NB):
        unit = jnp.where((side == 1) & (lane + k * W == goal), 1.0, 0.0)
        row = jnp.broadcast_to(load[0:1, k * W : (k + 1) * W], (8, W))
        tile = jnp.where(side == 0, row, unit)
        vec_out[8 * k : 8 * k + 8, :] = tile
        split[k] = split_rows(tile)
        vec.append(tile)
    small[0].wait()
    place01[...] = place_matrix(sep, (0, 1))
    place2[...] = place_matrix(sep, (2,))
    place34[...] = place_matrix(sep, (3, 4))
    for n, copy in enumerate(copies):
        copy.wait()
        for i in range(n * CHUNK, (n + 1) * CHUNK):
            store_split(raw[i], coupling, i)
        for i in range(n * CHUNK, (n + 1) * CHUNK):
            level, j = divmod(i, NB)
            put(payload, level, j, times_t(split[sep[level, j]], coupling[i]))
    small[2].wait()
    small[3].wait()
    for k in range(NB):
        store_split(raw_factor[k], factor, k)
    payload[LEVELS * ROWS :, :] = local_square(vec, pre_diag(shunt), 0.25, factor, inner_out)


def make_early_kernel(precond):
    def kernel(sum0, sum1, vec, inner, shunt, factor, coupling, place, acc):
        weights = PRE if precond else OP
        diag = pre_diag(shunt) if precond else own_diag(shunt)
        scale = 0.25 if precond else 1.0
        tiles = [
            diag[k] * tile_of(vec, k) + scale * times_t(inner[k], factor[k]) for k in range(NB)
        ]
        back = coarse_back((0, 1), (sum0, sum1), weights, coupling, place)
        acc[...] = back + jnp.concatenate(tiles, axis=0)

    return kernel


def make_middle_kernel(precond):
    def kernel(sum2, early, coupling, place, acc):
        weights = PRE if precond else OP
        acc[...] = early[...] + coarse_back((2,), (sum2,), weights, coupling, place)

    return kernel


def make_precond_kernel(first, last):
    def kernel(sep_vmem, sum3, sum4, square, middle, shunt, factor, coupling, flipped, place, *refs):
        if not first:
            old_direction, old_rho = refs[:2]
            refs = refs[2:]
        inner = None
        if not last:
            inner = refs[0]
            refs = refs[1:]
        payload, direction, rho, sep, split, sem = refs
        copy = pltpu.make_async_copy(sep_vmem, sep, sem)
        copy.start()
        acc = middle[...] + coarse_back((3, 4), (sum3, sum4), PRE, coupling, place)
        rho_new = side_totals(square)
        if not first:
            ratio = rho_new / old_rho[...]
        rho[...] = rho_new
        vec = []
        for k in range(NB):
            tile = acc[8 * k : 8 * k + 8]
            if not first:
                tile = tile + ratio * tile_of(old_direction, k)
            tile = keep_sides(tile)
            direction[8 * k : 8 * k + 8, :] = tile
            split[k] = split_rows(tile)
            vec.append(tile)
        copy.wait()
        contributions(flipped, sep, split, payload)
        payload[LEVELS * ROWS :, :] = local_square(vec, own_diag(shunt), 1.0, factor, inner)

    return kernel


def operator_kernel(
    sep_vmem,
    sum3,
    sum4,
    square,
    middle,
    shunt,
    factor,
    coupling,
    flipped,
    place,
    residual,
    rho,
    inner,
    payload,
    next_residual,
    step_out,
    sep,
    split,
    sem,
):
    copy = pltpu.make_async_copy(sep_vmem, sep, sem)
    copy.start()
    acc = middle[...] + coarse_back((3, 4), (sum3, sum4), OP, coupling, place)
    step = rho[...] / side_totals(square)
    step_out[...] = step
    vec = []
    for k in range(NB):
        tile = keep_sides(tile_of(residual, k) - step * acc[8 * k : 8 * k + 8])
        next_residual[8 * k : 8 * k + 8, :] = tile
        split[k] = split_rows(tile)
        vec.append(tile)
    payload[LEVELS * ROWS :, :] = local_square(vec, pre_diag(shunt), 0.25, factor, inner)
    copy.wait()
    contributions(flipped, sep, split, payload)


def make_update_kernel(first):
    def kernel(step, direction, *refs):
        for k in range(NB):
            tile = step[...] * tile_of(direction, k)
            if not first:
                tile = tile + tile_of(refs[0], k)
            refs[-1][8 * k : 8 * k + 8, :] = tile

    return kernel


def drops_kernel(vec, ends, drops):
    def chunk(i, carry):
        here = pl.ds(pl.multiple_of(8 * i, 8), 8)

        def at(end):
            index = ends[end, here, :]
            block = index >> 7
            lane = index & (W - 1)
            values = [jnp.zeros((8, W), F32)] * 2
            for k in range(NB):
                chosen = block == k
                for side in range(2):
                    row = jnp.broadcast_to(vec[8 * k + side : 8 * k + side + 1, :], (8, W))
                    found = jnp.take_along_axis(row, lane, axis=1)
                    values[side] = jnp.where(chosen, found, values[side])
            return values

        low, high = at(0), at(1)
        for side in range(2):
            drops[side, here, :] = low[side] - high[side]
        return carry

    lax.fori_loop(0, drops.shape[1] // 8, chunk, 0)


def last_kernel(square, direction, rho, estimate, known, change, volts, terms):
    step = rho[...] / side_totals(square)
    for side in range(2):
        gain = jnp.broadcast_to(step[side : side + 1, :], (8, W))
        if side == 0:
            forward = gain
        else:
            adjoint = gain
    for i in range(terms.shape[0] // 8):
        here = slice(8 * i, 8 * i + 8)
        drop = known[0, here, :] + forward * change[0, here, :]
        back = known[1, here, :] + adjoint * change[1, here, :]
        terms[here, :] = -(back * drop)
    for k in range(NB):
        tile = tile_of(estimate, k) + step * tile_of(direction, k)
        volts[0, k : k + 1, :] = tile[0:1]
        volts[1, k : k + 1, :] = tile[1:2]


TILES = jax.ShapeDtypeStruct((FLAT, W), F32)
PAYLOAD = jax.ShapeDtypeStruct((LEVELS * ROWS + 8, W), F32)
TILE = jax.ShapeDtypeStruct((8, W), F32)
INNER = jax.ShapeDtypeStruct((NB, 16, W), BF16)
COUPLING = jax.ShapeDtypeStruct((LEVELS * NB, 2 * W, W), BF16)
FACTOR = jax.ShapeDtypeStruct((NB, 2 * W, W), BF16)
PLACE = jax.ShapeDtypeStruct((FLAT, 256), BF16)
PLACE_TWO = jax.ShapeDtypeStruct((FLAT, 4 * FLAT), BF16)
SEP_SCRATCH = [
    pltpu.SMEM((LEVELS, NB), jnp.int32),
    pltpu.VMEM((NB, 16, W), BF16),
    pltpu.SemaphoreType.DMA,
]


def call(kernel, name, args, outs, scratch=(), hbm=(), limit=16):
    specs = [HBM if i in hbm else VMEM for i in range(len(args))]
    one = not isinstance(outs, list)
    return pl.pallas_call(
        kernel,
        in_specs=specs,
        out_specs=VMEM if one else [VMEM] * len(outs),
        out_shape=outs,
        scratch_shapes=list(scratch),
        compiler_params=pltpu.CompilerParams(vmem_limit_bytes=limit * MIB),
        name=name,
    )(*args)


OTHER_QUAD = {0: 6, 1: 7, 2: 4, 3: 5, 4: 2, 5: 3, 6: 0, 7: 1}


def partners(kind, count):
    if kind == "other":
        return [(s, s // 8 * 8 + OTHER_QUAD[s % 8]) for s in range(count)]
    return [(s, s ^ kind) for s in range(count)]


def power(rows):
    return rows[:8] * rows[:8] + rows[8:16] * rows[8:16] + rows[16:] * rows[16:]


def tree_exchange(payload, weights, jobs):
    count = lax.axis_size("dom")

    def fetch(value, kinds, number, finished, results):
        got = [lax.ppermute(value, "dom", partners(kind, count)) for kind in kinds]
        if number in jobs:
            results[number] = jobs[number](finished, results)
            got, results[number] = lax.optimization_barrier((got, results[number]))
            return got
        return lax.optimization_barrier(got)

    def quad(value, kinds, number, finished, results, level):
        farther, far, near = fetch(value, kinds, number, finished, results)
        pair = value[:-8] + near[:-8]
        other = far[:-8] + farther[:-8]
        low = pair[:ROWS]
        both = pair[ROWS:] + other[ROWS:]
        high = both[:ROWS]
        square = (value[-8:] + near[-8:]) + (far[-8:] + farther[-8:])
        square = square + weights[level] * (power(low) + power(other[:ROWS]))
        square = square + weights[level + 1] * power(high)
        return low, high, both[ROWS:], square

    results = {}
    low, high, pending, square = quad(payload, (3, 2, 1), 0, [], results, 0)
    finished = [low, high]
    pending = jnp.concatenate([pending, square], axis=0)
    (received,) = fetch(pending, ("other",), 1, finished, results)
    total = pending + received
    finished.append(total[:ROWS])
    square = total[-8:] + weights[2] * power(total[:ROWS])
    pending = jnp.concatenate([total[ROWS:-8], square], axis=0)
    low, high, _, square = quad(pending, (16, 24, 8), 2, finished, results, 3)
    return low, high, square, results


def shards(
    load_current, worst_node, cond_diag, branch, precond_factor, coupling, sep_map, strap_ends
):
    node_count = NB * W
    shunt = cond_diag.reshape(NB, W)
    target = worst_node - lax.axis_index("dom") * node_count
    target = jnp.broadcast_to(target[:, None], (1, W))
    ends = strap_ends.reshape(2, -1, W)
    strap_rows = ends.shape[1]
    drops_shape = jax.ShapeDtypeStruct(ends.shape, F32)

    payload, inner, residual, cpl, pre, place01, place2, place34 = call(
        first_kernel,
        "first_part",
        (
            pltpu.with_memory_space_constraint(sep_map, pltpu.HBM),
            target,
            pltpu.with_memory_space_constraint(load_current, pltpu.HBM),
            pltpu.with_memory_space_constraint(shunt, pltpu.HBM),
            pltpu.with_memory_space_constraint(coupling.reshape(LEVELS * NB, W, W), pltpu.HBM),
            pltpu.with_memory_space_constraint(precond_factor, pltpu.HBM),
        ),
        [PAYLOAD, INNER, TILES, COUPLING, FACTOR, PLACE_TWO, PLACE, PLACE_TWO],
        [
            pltpu.SMEM((LEVELS, NB), jnp.int32),
            pltpu.VMEM((1, node_count), F32),
            pltpu.VMEM((NB, W), F32),
            pltpu.VMEM((LEVELS * NB, W, W), F32),
            pltpu.VMEM((NB, W, W), F32),
            pltpu.VMEM((NB, 16, W), BF16),
            pltpu.SemaphoreType.DMA((4,)),
            pltpu.SemaphoreType.DMA((LEVELS * NB // CHUNK,)),
        ],
        hbm=(0, 2, 3, 4, 5),
        limit=24,
    )
    direction = rho = estimate = flipped = brn = step = None

    def exchange(payload, precond, vec, inner, factor, jobs, back=True):
        def early(finished, results):
            args = (finished[0], finished[1], vec, inner, shunt, factor, cpl, place01)
            return call(make_early_kernel(precond), "early_levels", args, TILES)

        def middle(finished, results):
            args = (finished[2], results[1], cpl, place2)
            return call(make_middle_kernel(precond), "middle_level", args, TILES)

        if back:
            jobs = {**jobs, 1: early, 2: middle}
        return tree_exchange(payload, PRE if precond else OP, jobs)

    for iteration in range(ITERS):
        first = iteration == 0
        last = iteration + 1 == ITERS
        jobs = {}
        if first:
            jobs[0] = lambda *_: (
                call(split_kernel, "split_branch", (branch,), FACTOR),
                call(transpose_kernel, "flip", (cpl,), COUPLING),
            )
        else:

            def update(*_):
                begun = () if estimate is None else (estimate,)
                args = (step, direction) + begun
                new = call(make_update_kernel(not begun), "update", args, TILES)
                if last:
                    return new, call(drops_kernel, "known", (new, ends), drops_shape)
                return (new,)

            jobs[0] = update
        sum3, sum4, square, results = exchange(payload, True, residual, inner, pre, jobs)
        if first:
            brn, flipped = results[0]
        else:
            estimate = results[0][0]
        if last:
            known = results[0][1]
        args = (sep_map, sum3, sum4, square, results[2], shunt, brn, cpl, flipped, place34)
        if not first:
            args += (direction, rho)
        outs = [PAYLOAD, TILES, TILE]
        *inner, payload, direction, rho = call(
            make_precond_kernel(first, last),
            "precond_round",
            args,
            outs if last else [INNER] + outs,
            SEP_SCRATCH,
        )
        inner = None if last else inner[0]
        jobs = {}
        if last:
            jobs[0] = lambda *_: call(drops_kernel, "change", (direction, ends), drops_shape)
        sum3, sum4, square, results = exchange(
            payload, False, direction, inner, brn, jobs, not last
        )
        if last:
            change = results[0]
        else:
            args = (sep_map, sum3, sum4, square, results[2], shunt, pre, cpl, flipped, place34)
            inner, payload, residual, step = call(
                operator_kernel,
                "operator_round",
                (*args, residual, rho),
                [INNER, PAYLOAD, TILES, TILE],
                SEP_SCRATCH,
            )
    volts, terms = call(
        last_kernel,
        "straps",
        (square, direction, rho, estimate, known, change),
        [
            jax.ShapeDtypeStruct((2, NB, W), F32),
            jax.ShapeDtypeStruct((strap_rows, W), F32),
        ],
    )
    terms = terms + lax.ppermute(terms, "load", [(s, s ^ 1) for s in range(8)])
    near, far, farther = [
        lax.ppermute(terms, "load", [(s, s ^ mask) for s in range(8)]) for mask in (2, 4, 6)
    ]
    terms = (terms + near) + (far + farther)
    return (volts.reshape(2, 1, node_count), terms.reshape(-1))


def solution(mesh):
    placed = (
        P("load", "dom"),
        P("load"),
        P("dom"),
        P("dom", None, None),
        P("dom", None, None),
        P(None, "dom", None, None),
        P(None, "dom"),
        P(None, "dom"),
    )
    return jax.shard_map(
        shards,
        mesh=mesh,
        in_specs=placed,
        out_specs=(P(None, "load", "dom"), P("dom")),
        check_vma=False,
    )
```

```python
import math

import jax
import jax.numpy as jnp
from jax import lax
from jax.experimental import pallas as pl
from jax.experimental.pallas import tpu as pltpu
from jax.sharding import PartitionSpec as P

ITERS = 4
LEVELS = 5
NB = 12
W = 128
ROWS = 2 * NB
FLAT = 8 * NB
CHUNK = 20
OP = [1.0 / math.sqrt(2.0 ** (level + 1)) for level in range(LEVELS)]
PRE = [0.5 * c for c in OP]
F32 = jnp.float32
BF16 = jnp.bfloat16
VMEM = pl.BlockSpec(memory_space=pltpu.VMEM)
HBM = pl.BlockSpec(memory_space=pltpu.HBM)
MIB = 1024 * 1024


def split_rows(tile):
    high = tile.astype(BF16).astype(F32)
    return jnp.concatenate([high, tile - high], axis=0).astype(BF16)


def times(rows, matrix):
    out = lax.dot_general(
        jnp.concatenate([rows, rows], axis=1),
        matrix,
        (((1,), (0,)), ((), ())),
        preferred_element_type=F32,
    )
    return out[:8] + out[8:]


def times_t(rows, matrix):
    out = lax.dot_general(rows, matrix, (((1,), (1,)), ((), ())), preferred_element_type=F32)
    out = out[:8] + out[8:]
    return out[:, :W] + out[:, W:]


def store_split(mats, out, index):
    high = mats.astype(BF16)
    out[index, :W, :] = high
    out[index, W:, :] = (mats - high.astype(F32)).astype(BF16)


def split_kernel(mat_ref, out_ref):
    for j in range(NB):
        store_split(mat_ref[j], out_ref, j)


def transpose_kernel(coupling, flipped):
    row = lax.broadcasted_iota(jnp.int32, (W, W), 0)
    eye = (row == lax.broadcasted_iota(jnp.int32, (W, W), 1)).astype(F32).astype(BF16)
    for i in range(LEVELS * NB):
        out = lax.dot_general(
            eye, coupling[i], (((1,), (1,)), ((), ())), preferred_element_type=F32
        ).astype(BF16)
        flipped[i, :W, :] = out[:, :W]
        flipped[i, W:, :] = out[:, W:]


def side_totals(square):
    total = square[...]
    total = total + pltpu.roll(total, 2, 0)
    total = total + pltpu.roll(total, 4, 0)
    return jnp.broadcast_to(jnp.sum(total, axis=1, keepdims=True), (8, W))


def keep_sides(tile):
    return jnp.where(lax.broadcasted_iota(jnp.int32, (8, W), 0) < 2, tile, 0.0)


def tile_of(ref, k):
    return ref[8 * k : 8 * k + 8, :]


def stacked(values):
    high = values.astype(BF16).astype(F32)
    parts = [high, values - high]
    spare = -2 * values.shape[0] % W
    if spare:
        parts.append(jnp.zeros((spare, W), F32))
    return jnp.concatenate(parts, axis=0).astype(BF16)


def dot(left, right):
    return lax.dot_general(left, right, (((1,), (0,)), ((), ())), preferred_element_type=F32)


def place_matrix(sep, levels):
    used = FLAT * len(levels)
    width = 2 * used + -2 * used % W
    row = lax.broadcasted_iota(jnp.int32, (8, width), 0)
    col = lax.broadcasted_iota(jnp.int32, (8, width), 1)
    inside = jnp.where(col >= used, col - used, col)
    number = jnp.where(inside >= FLAT, 1, 0)
    inside = inside - FLAT * number
    block = inside >> 3
    valid = (row < 2) & (col < 2 * used) & ((inside & 7) == 2 * (block & 3) + row)
    owner = jnp.full((8, width), -1, jnp.int32)
    for n, level in enumerate(levels):
        for j in range(NB):
            owner = jnp.where(valid & (number == n) & (block == j), sep[level, j], owner)
    tiles = [jnp.where(owner == k, 1.0, 0.0) for k in range(NB)]
    return jnp.concatenate(tiles, axis=0).astype(BF16)


def coarse_back(levels, totals, weights, coupling, place):
    outs = []
    for level, total in zip(levels, totals):
        for group in range(NB // 4):
            rows = split_rows(total[8 * group : 8 * group + 8, :] * weights[level])
            for member in range(4):
                outs.append(times(rows, coupling[level * NB + 4 * group + member]))
    return dot(place[...], stacked(jnp.concatenate(outs, axis=0)))


def local_square(vec, diag, scale, factor, inner_out):
    square = jnp.zeros((8, W), F32)
    for k in range(NB):
        inner = times(split_rows(vec[k]), factor[k])
        if inner_out is not None:
            inner_out[k] = split_rows(inner)
        square = square + (diag[k] * vec[k] * vec[k] + scale * (inner * inner))
    return square


def put(payload, level, j, out):
    payload[level * ROWS + 2 * j : level * ROWS + 2 * j + 2, :] = out[0:2]


def contributions(flipped, sep, split, payload):
    for level in range(LEVELS):
        for j in range(NB):
            put(payload, level, j, times(split[sep[level, j]], flipped[level * NB + j]))


def own_diag(shunt):
    return [jnp.broadcast_to(shunt[k : k + 1, :], (8, W)) for k in range(NB)]


def pre_diag(shunt):
    return [1.0 / (tile + 1.0) for tile in own_diag(shunt)]


def first_kernel(
    sep_hbm,
    target,
    load_hbm,
    shunt_hbm,
    coupling_hbm,
    factor_hbm,
    payload,
    inner_out,
    vec_out,
    coupling,
    factor,
    place01,
    place2,
    place34,
    sep,
    load,
    shunt,
    raw,
    raw_factor,
    split,
    small_sems,
    sems,
):
    small = [
        pltpu.make_async_copy(source, place, small_sems.at[n])
        for n, (source, place) in enumerate(
            ((sep_hbm, sep), (load_hbm, load), (shunt_hbm, shunt), (factor_hbm, raw_factor))
        )
    ]
    copies = [
        pltpu.make_async_copy(
            coupling_hbm.at[pl.ds(n * CHUNK, CHUNK)], raw.at[pl.ds(n * CHUNK, CHUNK)], sems.at[n]
        )
        for n in range(LEVELS * NB // CHUNK)
    ]
    for copy in small[:3] + copies + small[3:]:
        copy.start()
    small[1].wait()
    side = lax.broadcasted_iota(jnp.int32, (8, W), 0)
    lane = lax.broadcasted_iota(jnp.int32, (8, W), 1)
    goal = jnp.broadcast_to(target[...], (8, W))
    vec = []
    for k in range(NB):
        unit = jnp.where((side == 1) & (lane + k * W == goal), 1.0, 0.0)
        row = jnp.broadcast_to(load[0:1, k * W : (k + 1) * W], (8, W))
        tile = jnp.where(side == 0, row, unit)
        vec_out[8 * k : 8 * k + 8, :] = tile
        split[k] = split_rows(tile)
        vec.append(tile)
    small[0].wait()
    place01[...] = place_matrix(sep, (0, 1))
    place2[...] = place_matrix(sep, (2,))
    place34[...] = place_matrix(sep, (3, 4))
    for n, copy in enumerate(copies):
        copy.wait()
        for i in range(n * CHUNK, (n + 1) * CHUNK):
            store_split(raw[i], coupling, i)
        for i in range(n * CHUNK, (n + 1) * CHUNK):
            level, j = divmod(i, NB)
            put(payload, level, j, times_t(split[sep[level, j]], coupling[i]))
    small[2].wait()
    small[3].wait()
    for k in range(NB):
        store_split(raw_factor[k], factor, k)
    payload[LEVELS * ROWS :, :] = local_square(vec, pre_diag(shunt), 0.25, factor, inner_out)


def make_early_kernel(precond):
    def kernel(sum0, sum1, vec, inner, shunt, factor, coupling, place, acc):
        weights = PRE if precond else OP
        diag = pre_diag(shunt) if precond else own_diag(shunt)
        scale = 0.25 if precond else 1.0
        tiles = [
            diag[k] * tile_of(vec, k) + scale * times_t(inner[k], factor[k]) for k in range(NB)
        ]
        back = coarse_back((0, 1), (sum0, sum1), weights, coupling, place)
        acc[...] = back + jnp.concatenate(tiles, axis=0)

    return kernel


def make_middle_kernel(precond):
    def kernel(sum2, early, coupling, place, acc):
        weights = PRE if precond else OP
        acc[...] = early[...] + coarse_back((2,), (sum2,), weights, coupling, place)

    return kernel


def make_precond_kernel(first, last):
    def kernel(sep_vmem, sum3, sum4, square, middle, shunt, factor, coupling, flipped, place, *refs):
        if not first:
            old_direction, old_rho = refs[:2]
            refs = refs[2:]
        inner = None
        if not last:
            inner = refs[0]
            refs = refs[1:]
        payload, direction, rho, sep, split, sem = refs
        copy = pltpu.make_async_copy(sep_vmem, sep, sem)
        copy.start()
        acc = middle[...] + coarse_back((3, 4), (sum3, sum4), PRE, coupling, place)
        rho_new = side_totals(square)
        if not first:
            ratio = rho_new / old_rho[...]
        rho[...] = rho_new
        vec = []
        for k in range(NB):
            tile = acc[8 * k : 8 * k + 8]
            if not first:
                tile = tile + ratio * tile_of(old_direction, k)
            tile = keep_sides(tile)
            direction[8 * k : 8 * k + 8, :] = tile
            split[k] = split_rows(tile)
            vec.append(tile)
        copy.wait()
        contributions(flipped, sep, split, payload)
        payload[LEVELS * ROWS :, :] = local_square(vec, own_diag(shunt), 1.0, factor, inner)

    return kernel


def operator_kernel(
    sep_vmem,
    sum3,
    sum4,
    square,
    middle,
    shunt,
    factor,
    coupling,
    flipped,
    place,
    residual,
    rho,
    inner,
    payload,
    next_residual,
    step_out,
    sep,
    split,
    sem,
):
    copy = pltpu.make_async_copy(sep_vmem, sep, sem)
    copy.start()
    acc = middle[...] + coarse_back((3, 4), (sum3, sum4), OP, coupling, place)
    step = rho[...] / side_totals(square)
    step_out[...] = step
    vec = []
    for k in range(NB):
        tile = keep_sides(tile_of(residual, k) - step * acc[8 * k : 8 * k + 8])
        next_residual[8 * k : 8 * k + 8, :] = tile
        split[k] = split_rows(tile)
        vec.append(tile)
    payload[LEVELS * ROWS :, :] = local_square(vec, pre_diag(shunt), 0.25, factor, inner)
    copy.wait()
    contributions(flipped, sep, split, payload)


def make_update_kernel(first):
    def kernel(step, direction, *refs):
        for k in range(NB):
            tile = step[...] * tile_of(direction, k)
            if not first:
                tile = tile + tile_of(refs[0], k)
            refs[-1][8 * k : 8 * k + 8, :] = tile

    return kernel


def drops_kernel(vec, ends, drops):
    def chunk(i, carry):
        here = pl.ds(pl.multiple_of(8 * i, 8), 8)

        def at(end):
            index = ends[end, here, :]
            block = index >> 7
            lane = index & (W - 1)
            values = [jnp.zeros((8, W), F32)] * 2
            for k in range(NB):
                chosen = block == k
                for side in range(2):
                    row = jnp.broadcast_to(vec[8 * k + side : 8 * k + side + 1, :], (8, W))
                    found = jnp.take_along_axis(row, lane, axis=1)
                    values[side] = jnp.where(chosen, found, values[side])
            return values

        low, high = at(0), at(1)
        for side in range(2):
            drops[side, here, :] = low[side] - high[side]
        return carry

    lax.fori_loop(0, drops.shape[1] // 8, chunk, 0)


def last_kernel(square, direction, rho, estimate, known, change, volts, terms):
    step = rho[...] / side_totals(square)
    for side in range(2):
        gain = jnp.broadcast_to(step[side : side + 1, :], (8, W))
        if side == 0:
            forward = gain
        else:
            adjoint = gain
    for i in range(terms.shape[0] // 8):
        here = slice(8 * i, 8 * i + 8)
        drop = known[0, here, :] + forward * change[0, here, :]
        back = known[1, here, :] + adjoint * change[1, here, :]
        terms[here, :] = -(back * drop)
    for k in range(NB):
        tile = tile_of(estimate, k) + step * tile_of(direction, k)
        volts[0, k : k + 1, :] = tile[0:1]
        volts[1, k : k + 1, :] = tile[1:2]


TILES = jax.ShapeDtypeStruct((FLAT, W), F32)
PAYLOAD = jax.ShapeDtypeStruct((LEVELS * ROWS + 8, W), F32)
TILE = jax.ShapeDtypeStruct((8, W), F32)
INNER = jax.ShapeDtypeStruct((NB, 16, W), BF16)
COUPLING = jax.ShapeDtypeStruct((LEVELS * NB, 2 * W, W), BF16)
FACTOR = jax.ShapeDtypeStruct((NB, 2 * W, W), BF16)
PLACE = jax.ShapeDtypeStruct((FLAT, 256), BF16)
PLACE_TWO = jax.ShapeDtypeStruct((FLAT, 4 * FLAT), BF16)
SEP_SCRATCH = [
    pltpu.SMEM((LEVELS, NB), jnp.int32),
    pltpu.VMEM((NB, 16, W), BF16),
    pltpu.SemaphoreType.DMA,
]


def call(kernel, name, args, outs, scratch=(), hbm=(), limit=16):
    specs = [HBM if i in hbm else VMEM for i in range(len(args))]
    one = not isinstance(outs, list)
    return pl.pallas_call(
        kernel,
        in_specs=specs,
        out_specs=VMEM if one else [VMEM] * len(outs),
        out_shape=outs,
        scratch_shapes=list(scratch),
        compiler_params=pltpu.CompilerParams(vmem_limit_bytes=limit * MIB),
        name=name,
    )(*args)


OTHER_QUAD = {0: 6, 1: 7, 2: 4, 3: 5, 4: 2, 5: 3, 6: 0, 7: 1}


def partners(kind, count):
    if kind == "other":
        return [(s, s // 8 * 8 + OTHER_QUAD[s % 8]) for s in range(count)]
    return [(s, s ^ kind) for s in range(count)]


def power(rows):
    return rows[:8] * rows[:8] + rows[8:16] * rows[8:16] + rows[16:] * rows[16:]


def tree_exchange(payload, weights, jobs):
    count = lax.axis_size("dom")

    def fetch(value, kinds, number, finished, results):
        got = [lax.ppermute(value, "dom", partners(kind, count)) for kind in kinds]
        if number in jobs:
            results[number] = jobs[number](finished, results)
            got, results[number] = lax.optimization_barrier((got, results[number]))
            return got
        return lax.optimization_barrier(got)

    def quad(value, kinds, number, finished, results, level):
        farther, far, near = fetch(value, kinds, number, finished, results)
        pair = value[:-8] + near[:-8]
        other = far[:-8] + farther[:-8]
        low = pair[:ROWS]
        both = pair[ROWS:] + other[ROWS:]
        high = both[:ROWS]
        square = (value[-8:] + near[-8:]) + (far[-8:] + farther[-8:])
        square = square + weights[level] * (power(low) + power(other[:ROWS]))
        square = square + weights[level + 1] * power(high)
        return low, high, both[ROWS:], square

    results = {}
    low, high, pending, square = quad(payload, (2, 3, 1), 0, [], results, 0)
    finished = [low, high]
    pending = jnp.concatenate([pending, square], axis=0)
    (received,) = fetch(pending, ("other",), 1, finished, results)
    total = pending + received
    finished.append(total[:ROWS])
    square = total[-8:] + weights[2] * power(total[:ROWS])
    pending = jnp.concatenate([total[ROWS:-8], square], axis=0)
    low, high, _, square = quad(pending, (16, 24, 8), 2, finished, results, 3)
    return low, high, square, results


def shards(
    load_current, worst_node, cond_diag, branch, precond_factor, coupling, sep_map, strap_ends
):
    node_count = NB * W
    shunt = cond_diag.reshape(NB, W)
    target = worst_node - lax.axis_index("dom") * node_count
    target = jnp.broadcast_to(target[:, None], (1, W))
    ends = strap_ends.reshape(2, -1, W)
    strap_rows = ends.shape[1]
    drops_shape = jax.ShapeDtypeStruct(ends.shape, F32)

    payload, inner, residual, cpl, pre, place01, place2, place34 = call(
        first_kernel,
        "first_part",
        (
            pltpu.with_memory_space_constraint(sep_map, pltpu.HBM),
            target,
            pltpu.with_memory_space_constraint(load_current, pltpu.HBM),
            pltpu.with_memory_space_constraint(shunt, pltpu.HBM),
            pltpu.with_memory_space_constraint(coupling.reshape(LEVELS * NB, W, W), pltpu.HBM),
            pltpu.with_memory_space_constraint(precond_factor, pltpu.HBM),
        ),
        [PAYLOAD, INNER, TILES, COUPLING, FACTOR, PLACE_TWO, PLACE, PLACE_TWO],
        [
            pltpu.SMEM((LEVELS, NB), jnp.int32),
            pltpu.VMEM((1, node_count), F32),
            pltpu.VMEM((NB, W), F32),
            pltpu.VMEM((LEVELS * NB, W, W), F32),
            pltpu.VMEM((NB, W, W), F32),
            pltpu.VMEM((NB, 16, W), BF16),
            pltpu.SemaphoreType.DMA((4,)),
            pltpu.SemaphoreType.DMA((LEVELS * NB // CHUNK,)),
        ],
        hbm=(0, 2, 3, 4, 5),
        limit=24,
    )
    direction = rho = estimate = flipped = brn = step = None

    def exchange(payload, precond, vec, inner, factor, jobs, back=True):
        def early(finished, results):
            args = (finished[0], finished[1], vec, inner, shunt, factor, cpl, place01)
            return call(make_early_kernel(precond), "early_levels", args, TILES)

        def middle(finished, results):
            args = (finished[2], results[1], cpl, place2)
            return call(make_middle_kernel(precond), "middle_level", args, TILES)

        if back:
            jobs = {**jobs, 1: early, 2: middle}
        return tree_exchange(payload, PRE if precond else OP, jobs)

    for iteration in range(ITERS):
        first = iteration == 0
        last = iteration + 1 == ITERS
        jobs = {}
        if first:
            jobs[0] = lambda *_: (
                call(split_kernel, "split_branch", (branch,), FACTOR),
                call(transpose_kernel, "flip", (cpl,), COUPLING),
            )
        else:

            def update(*_):
                begun = () if estimate is None else (estimate,)
                args = (step, direction) + begun
                new = call(make_update_kernel(not begun), "update", args, TILES)
                if last:
                    return new, call(drops_kernel, "known", (new, ends), drops_shape)
                return (new,)

            jobs[0] = update
        sum3, sum4, square, results = exchange(payload, True, residual, inner, pre, jobs)
        if first:
            brn, flipped = results[0]
        else:
            estimate = results[0][0]
        if last:
            known = results[0][1]
        args = (sep_map, sum3, sum4, square, results[2], shunt, brn, cpl, flipped, place34)
        if not first:
            args += (direction, rho)
        outs = [PAYLOAD, TILES, TILE]
        *inner, payload, direction, rho = call(
            make_precond_kernel(first, last),
            "precond_round",
            args,
            outs if last else [INNER] + outs,
            SEP_SCRATCH,
        )
        inner = None if last else inner[0]
        jobs = {}
        if last:
            jobs[0] = lambda *_: call(drops_kernel, "change", (direction, ends), drops_shape)
        sum3, sum4, square, results = exchange(
            payload, False, direction, inner, brn, jobs, not last
        )
        if last:
            change = results[0]
        else:
            args = (sep_map, sum3, sum4, square, results[2], shunt, pre, cpl, flipped, place34)
            inner, payload, residual, step = call(
                operator_kernel,
                "operator_round",
                (*args, residual, rho),
                [INNER, PAYLOAD, TILES, TILE],
                SEP_SCRATCH,
            )
    volts, terms = call(
        last_kernel,
        "straps",
        (square, direction, rho, estimate, known, change),
        [
            jax.ShapeDtypeStruct((2, NB, W), F32),
            jax.ShapeDtypeStruct((strap_rows, W), F32),
        ],
    )
    terms = terms + lax.ppermute(terms, "load", [(s, s ^ 1) for s in range(8)])
    near, far, farther = [
        lax.ppermute(terms, "load", [(s, s ^ mask) for s in range(8)]) for mask in (2, 4, 6)
    ]
    terms = (terms + near) + (far + farther)
    return (volts.reshape(2, 1, node_count), terms.reshape(-1))


def solution(mesh):
    placed = (
        P("load", "dom"),
        P("load"),
        P("dom"),
        P("dom", None, None),
        P("dom", None, None),
        P(None, "dom", None, None),
        P(None, "dom"),
        P(None, "dom"),
    )
    return jax.shard_map(
        shards,
        mesh=mesh,
        in_specs=placed,
        out_specs=(P(None, "load", "dom"), P("dom")),
        check_vma=False,
    )
```
